32 devices in a mesh: section: 4 (over z), dp: 4 (over y, core), mp: 2 (over x).
Axes of the slice: x: 2, y: 2, z: 4, core: 2. Of those that a mesh axis runs over, the one named last changes fastest.
Arguments:
- enc_rows: bfloat16 [4096, 4096], P(('section', 'dp'), 'mp'), may hold values from -6 to 6
- enc_len: int32 [64], P(('section', 'dp')), may hold values from 16 to 64
- dest_dp: int32 [64], P(('section', 'dp')), may hold values from 0 to 3, as said below
- peer_counts: int32 [16, 4], P(('section', 'dp')), may hold values from 0 to 2, as said below
- queries: bfloat16 [4096, 4096], P(('section', 'dp'), 'mp'), may hold values from -50 to 50
- ctx_grad: bfloat16 [4096, 4096], P(('section', 'dp'), 'mp'), may hold values from -6 to 6
- w_key: bfloat16 [4096, 4096], P(('section', 'dp'), 'mp'), may hold values from -0.09375 to 0.09375
- w_value: bfloat16 [4096, 4096], P(('section', 'dp'), 'mp'), may hold values from -0.09375 to 0.09375
Outputs:
- context: bfloat16 [4096, 4096], P(('section', 'dp'), 'mp')
- enc_grad: bfloat16 [4096, 4096], P(('section', 'dp'), 'mp')
The draws below stay inside these ranges and needn't reach their ends.
Inputs may be any that keep to these rules, and one draw needn't show every extreme that they name: `dest_dp`: each device places at most 2 of its blocks on one decoder device of its section, some device exactly 2, and every device takes exactly 4 blocks. peer_counts agrees with dest_dp; each row sums to 4.
All inputs are finite; a program needn't handle non-finite values.
Results may differ from the reference program's by a relative error of at most 0.014.
Values may be sent and summed in bfloat16 or wider, within the bound.
No kernel may reach another device: no remote copies, remote signals or barrier semaphores. Data moves between devices by JAX's collectives and lax.ppermute only.
A program may use at most 128 MiB of HBM per device.

```python
import math
import jax
import jax.numpy as jnp
from jax import lax

D = 4096
DH = 64
BLOCK = 64
BLK_DEV = 4
CAP = 2
INNER = 4096
N_BLK = 64
ROWS = 4096
N_SECTION = 4
N_DP = 4
N_MP = 2


def placement_tables(key):
    folded = jax.random.fold_in(key, 4242)
    label_key, offset_key, shuffle_key = jax.random.split(folded, 3)
    relabel = jax.vmap(lambda subkey: jax.random.permutation(subkey, N_DP))(jax.random.split(label_key, N_SECTION)).astype(jnp.int32)
    offset_perm = jax.vmap(lambda subkey: jax.random.permutation(subkey, N_DP))(jax.random.split(offset_key, N_SECTION)).astype(jnp.int32)
    positions = jnp.arange(BLK_DEV, dtype=jnp.int32)
    offset_pick = jnp.where(positions < CAP, 0, 1 + (positions - CAP) % max(N_DP - 1, 1)).astype(jnp.int32)
    offsets = offset_perm[:, offset_pick]
    inverse = jnp.argsort(relabel, axis=1).astype(jnp.int32)
    target_pos = (inverse[:, :, None] + offsets[:, None, :]) % N_DP
    destinations = jax.vmap(lambda relabel_row, target_row: relabel_row[target_row])(relabel, target_pos)
    shuffles = jax.vmap(lambda subkey: jax.random.permutation(subkey, BLK_DEV))(jax.random.split(shuffle_key, N_SECTION * N_DP))
    shuffles = shuffles.reshape(N_SECTION, N_DP, BLK_DEV).astype(jnp.int32)
    destinations = jnp.take_along_axis(destinations, shuffles, axis=2).astype(jnp.int32)
    dp_ids = jnp.arange(N_DP, dtype=jnp.int32)
    arrivals = jnp.sum((destinations[:, None, :, :] == dp_ids[None, :, None, None]).astype(jnp.int32), axis=3)
    return (destinations.reshape(-1).astype(jnp.int32), arrivals.reshape(N_SECTION * N_DP, N_DP).astype(jnp.int32))


def draw_dest_dp(key, part):
    return placement_tables(key)[0]


def draw_peer_counts(key, part):
    return placement_tables(key)[1]


def draw_queries(key, part):
    noise_key, scale_key = jax.random.split(jax.random.fold_in(key, 11), 2)
    noise = jnp.clip(jax.random.normal(noise_key, (ROWS, INNER), jnp.float32), -4.0, 4.0)
    row_scale = jnp.exp(jax.random.uniform(scale_key, (ROWS, 1), jnp.float32, 0.0, math.log(3.0)))
    return (noise * row_scale).astype(jnp.bfloat16)


def place_ends(drawn, own_key, low, largest):
    shape = drawn.shape
    index_at = [jax.random.randint(jax.random.fold_in(own_key, axis), (), 0, shape[axis]) for axis in range(len(shape))]
    drawn = drawn.at[tuple(index_at)].set(low)
    longest = shape.index(max(shape))
    index_at[longest] = (index_at[longest] + 1) % shape[longest]
    return drawn.at[tuple(index_at)].set(largest)


def shard_levels(stream_key, shape, cuts, least, top_value):
    gain = 1.0
    for axis_at, shards_of in cuts:
        steps = jax.random.uniform(jax.random.fold_in(jax.random.fold_in(stream_key, 6), axis_at), (shards_of,), jnp.float32, least / len(cuts), top_value / len(cuts))
        gain = gain * jnp.repeat(jnp.exp(steps), shape[axis_at] // shards_of).reshape((-1,) + (1,) * (len(shape) - 1 - axis_at))
    return gain


def bell_draw(rng, extent, spread, bound, shards=(), kind=jnp.bfloat16):
    result = spread * jax.random.normal(rng, extent, jnp.float32)
    if shards:
        result = result * shard_levels(rng, extent, shards, -0.22, 0.18)
    return jnp.clip(result, -bound, bound).astype(kind)


def setup_inputs(seed: int = 0) -> dict:
    key_list = jax.random.split(jax.random.key(seed), 9)
    return {
        "enc_rows": bell_draw(key_list[0], (ROWS, D), 1.0, 6.0, ((0, 16), (1, 2))),
        "enc_len": place_ends(jax.random.randint(key_list[1], (N_BLK,), BLOCK // 4, BLOCK + 1), jax.random.fold_in(key_list[1], 1), BLOCK // 4, BLOCK).astype(jnp.int32),
        "dest_dp": draw_dest_dp(jax.random.fold_in(key_list[8], 71), 0),
        "peer_counts": draw_peer_counts(jax.random.fold_in(key_list[8], 71), 0),
        "queries": draw_queries(jax.random.fold_in(key_list[8], 71), 0),
        "ctx_grad": bell_draw(key_list[5], (ROWS, INNER), 1.0, 6.0, ((0, 16), (1, 2))),
        "w_key": bell_draw(key_list[6], (D, INNER), D ** -0.5, 0.09375, ((0, 16), (1, 2))),
        "w_value": bell_draw(key_list[7], (D, INNER), D ** -0.5, 0.09375, ((0, 16), (1, 2))),
    }


def attend(query_rows, key_rows, value_rows, grad_rows, key_lengths):
    block_count = key_lengths.shape[0]
    head_count = query_rows.shape[1] // DH
    shape_four = (block_count, BLOCK, head_count, DH)
    query_heads = query_rows.astype(jnp.float32).reshape(shape_four)
    key_heads = key_rows.astype(jnp.float32).reshape(shape_four)
    value_heads = value_rows.astype(jnp.float32).reshape(shape_four)
    grad_heads = grad_rows.astype(jnp.float32).reshape(shape_four)
    score_scale = DH ** -0.5
    scores = jnp.einsum("bihd,bjhd->bhij", query_heads, key_heads) * score_scale
    visible = jnp.arange(BLOCK, dtype=jnp.int32)[None, None, None, :] < key_lengths.astype(jnp.int32)[:, None, None, None]
    scores = jnp.where(visible, scores, -1e30)
    row_max = jnp.max(scores, axis=-1, keepdims=True)
    weights_exp = jnp.exp(scores - row_max)
    probabilities = weights_exp / jnp.sum(weights_exp, axis=-1, keepdims=True)
    prob_bf = lax.optimization_barrier(probabilities.astype(jnp.bfloat16)).astype(jnp.float32)
    context = jnp.einsum("bhij,bjhd->bihd", prob_bf, value_heads).astype(jnp.bfloat16)
    prob_grad = jnp.einsum("bihd,bjhd->bhij", grad_heads, value_heads)
    row_dot = jnp.sum(probabilities * prob_grad, axis=-1, keepdims=True)
    score_grad = probabilities * (prob_grad - row_dot) * score_scale
    score_grad = lax.optimization_barrier(score_grad.astype(jnp.bfloat16)).astype(jnp.float32)
    key_grad = jnp.einsum("bhij,bihd->bjhd", score_grad, query_heads).astype(jnp.bfloat16)
    value_grad = jnp.einsum("bhij,bihd->bjhd", prob_bf, grad_heads).astype(jnp.bfloat16)
    flat_shape = (block_count * BLOCK, head_count * DH)
    return context.reshape(flat_shape), key_grad.reshape(flat_shape), value_grad.reshape(flat_shape)


def reference(enc_rows, enc_len, dest_dp, peer_counts, queries, ctx_grad, w_key, w_value):
    device_groups = N_SECTION * N_DP
    group_width = INNER // N_MP
    destinations = dest_dp.reshape(N_SECTION, N_DP, BLK_DEV)
    device_ids = jnp.arange(device_groups, dtype=jnp.int32)
    section_of = (device_ids // N_DP).astype(jnp.int32)
    dp_of = (device_ids % N_DP).astype(jnp.int32)
    positions = jnp.arange(BLK_DEV, dtype=jnp.int32)
    arrival_ends = jnp.cumsum(peer_counts, axis=1).astype(jnp.int32)
    sender = jnp.sum((arrival_ends[:, None, :] <= positions[None, :, None]).astype(jnp.int32), axis=2).astype(jnp.int32)
    first_pos = (jnp.take_along_axis(arrival_ends, sender, axis=1) - jnp.take_along_axis(peer_counts, sender, axis=1)).astype(jnp.int32)
    rank_want = (positions[None, :] - first_pos).astype(jnp.int32)
    sender_lists = destinations[section_of[:, None], sender]
    matches = sender_lists == dp_of[:, None, None]
    slot_rank = jnp.cumsum(matches.astype(jnp.int32), axis=2).astype(jnp.int32) - 1
    chosen = matches & (slot_rank == rank_want[:, :, None])
    chosen_block = jnp.sum(jnp.where(chosen, positions[None, None, :], 0), axis=2).astype(jnp.int32)
    src_blk = ((section_of[:, None] * N_DP + sender) * BLK_DEV + chosen_block).astype(jnp.int32)

    enc_blocks = enc_rows.reshape(N_BLK, BLOCK, D)
    query_blocks = queries.reshape(device_groups, BLK_DEV * BLOCK, INNER)
    grad_blocks = ctx_grad.reshape(device_groups, BLK_DEV * BLOCK, INNER)
    key_weights = w_key.astype(jnp.float32).reshape(D, N_MP, group_width)
    value_weights = w_value.astype(jnp.float32).reshape(D, N_MP, group_width)

    def per_device(operands):
        sources, query_rows, grad_rows = operands
        enc_block = jnp.take(enc_blocks, sources, axis=0).reshape(BLK_DEV * BLOCK, D)
        key_lengths = jnp.take(enc_len, sources, axis=0)
        key_rows = lax.optimization_barrier(jnp.dot(enc_block, w_key, preferred_element_type=jnp.float32).astype(jnp.bfloat16))
        value_rows = lax.optimization_barrier(jnp.dot(enc_block, w_value, preferred_element_type=jnp.float32).astype(jnp.bfloat16))
        context, key_grad, value_grad = attend(query_rows, key_rows, value_rows, grad_rows, key_lengths)
        key_split = key_grad.astype(jnp.float32).reshape(-1, N_MP, group_width)
        value_split = value_grad.astype(jnp.float32).reshape(-1, N_MP, group_width)
        partial_value = jnp.einsum("rmi,dmi->mrd", key_split, key_weights) + jnp.einsum("rmi,dmi->mrd", value_split, value_weights)
        partial_value = lax.optimization_barrier(partial_value.astype(jnp.bfloat16)).astype(jnp.float32)
        grad_out = jnp.sum(partial_value, axis=0).astype(jnp.bfloat16)
        return context, grad_out.reshape(BLK_DEV, BLOCK, D)

    contexts, grads = lax.map(per_device, (src_blk, query_blocks, grad_blocks))
    enc_grad = jnp.zeros((N_BLK, BLOCK, D), jnp.bfloat16).at[src_blk.reshape(-1)].set(grads.reshape(N_BLK, BLOCK, D))
    return contexts.reshape(ROWS, INNER), enc_grad.reshape(ROWS, D)
```

```python
import functools

import jax
import jax.numpy as jnp
from jax import lax
from jax.experimental import pallas as pl
from jax.experimental.pallas import tpu as pltpu
from jax.sharding import PartitionSpec as P

DH = 64
BLOCK = 64
F32 = jnp.float32
BF16 = jnp.bfloat16


def attend(query_rows, key_rows, value_rows, grad_rows, key_lengths):
    block_count = key_lengths.shape[0]
    head_count = query_rows.shape[1] // DH
    shape_four = (block_count, BLOCK, head_count, DH)
    query_heads = query_rows.reshape(shape_four)
    key_heads = key_rows.reshape(shape_four)
    value_heads = value_rows.reshape(shape_four)
    grad_heads = grad_rows.reshape(shape_four)
    score_scale = DH ** (-0.5)
    scores = (
        jnp.einsum("bihd,bjhd->bhij", query_heads, key_heads, preferred_element_type=jnp.float32)
        * score_scale
    )
    visible = (
        jnp.arange(BLOCK, dtype=jnp.float32)[None, None, None, :] < key_lengths[:, None, None, None]
    )
    scores = jnp.where(visible, scores, -1e30)
    row_max = jnp.max(scores, axis=-1, keepdims=True)
    weights_exp = jnp.exp(scores - row_max)
    probabilities = weights_exp / jnp.sum(weights_exp, axis=-1, keepdims=True)
    prob_bf = probabilities.astype(jnp.bfloat16)
    context = jnp.einsum(
        "bhij,bjhd->bihd", prob_bf, value_heads, preferred_element_type=jnp.float32
    ).astype(jnp.bfloat16)
    prob_grad = jnp.einsum(
        "bihd,bjhd->bhij", grad_heads, value_heads, preferred_element_type=jnp.float32
    )
    row_dot = jnp.sum(probabilities * prob_grad, axis=-1, keepdims=True)
    score_grad = (probabilities * (prob_grad - row_dot) * score_scale).astype(jnp.bfloat16)
    key_grad = jnp.einsum(
        "bhij,bihd->bjhd", score_grad, query_heads, preferred_element_type=jnp.float32
    ).astype(jnp.bfloat16)
    value_grad = jnp.einsum(
        "bhij,bihd->bjhd", prob_bf, grad_heads, preferred_element_type=jnp.float32
    ).astype(jnp.bfloat16)
    flat_shape = (block_count * BLOCK, head_count * DH)
    return (
        context.reshape(flat_shape),
        key_grad.reshape(flat_shape),
        value_grad.reshape(flat_shape),
    )


def through(table, data, lead_shape):
    moved = jnp.dot(table, data, preferred_element_type=jnp.float32).astype(jnp.bfloat16)
    return moved.reshape(lead_shape + data.shape[1:])


def shards_general(enc_rows, enc_len, dest_dp, peer_counts, queries, ctx_grad, w_key, w_value):
    peer_count = lax.axis_size("dp")
    model_groups = lax.axis_size("mp")
    block_count = dest_dp.shape[0]
    slot_count = max(2, -(-block_count // peer_count))
    row_count, feature_width = enc_rows.shape
    key_full, value_full = (
        lax.all_gather(w_key, ("section", "dp"), axis=0, tiled=True),
        lax.all_gather(w_value, ("section", "dp"), axis=0, tiled=True),
    )
    positions = jnp.arange(block_count, dtype=jnp.int32)
    same_dest = dest_dp[:, None] == dest_dp[None, :]
    slot_rank = jnp.sum(
        (same_dest & (positions[None, :] < positions[:, None])).astype(jnp.int32), axis=1
    )
    target_slot = dest_dp * slot_count + slot_rank
    slot_ids = jnp.arange(peer_count * slot_count, dtype=jnp.int32)
    send_map = (slot_ids[:, None] == target_slot[None, :]).astype(jnp.bfloat16)
    arrivals = peer_counts[0]
    arrival_ends = jnp.cumsum(arrivals)
    sender = jnp.sum((arrival_ends[None, :] <= positions[:, None]).astype(jnp.int32), axis=1)
    first_pos = jnp.take(arrival_ends, sender) - jnp.take(arrivals, sender)
    slot_pick = sender * slot_count + positions - first_pos
    recv_map = (slot_pick[:, None] == slot_ids[None, :]).astype(jnp.bfloat16)
    lengths_own = enc_len.astype(jnp.float32).astype(jnp.bfloat16).reshape(block_count, 1)
    all_slots = peer_count * slot_count
    outgoing = through(send_map, enc_rows.reshape(block_count, -1), (peer_count, slot_count))
    outgoing_len = through(send_map, lengths_own, (peer_count, slot_count))
    incoming, incoming_len = (
        lax.all_to_all(outgoing, "dp", split_axis=0, concat_axis=0, tiled=True),
        lax.all_to_all(outgoing_len, "dp", split_axis=0, concat_axis=0, tiled=True),
    )
    rows_here = through(recv_map, incoming.reshape(all_slots, -1), (block_count,)).reshape(
        row_count, feature_width
    )
    lengths_here = through(recv_map, incoming_len.reshape(all_slots, 1), (block_count,))[
        :, 0
    ].astype(jnp.float32)
    shard_cols = lax.all_gather(rows_here, "mp", axis=1, tiled=True)
    key_acc = jnp.dot(shard_cols, key_full, preferred_element_type=jnp.float32)
    value_acc = jnp.dot(shard_cols, value_full, preferred_element_type=jnp.float32)
    context, key_grad, value_grad = attend(
        queries,
        key_acc.astype(jnp.bfloat16),
        value_acc.astype(jnp.bfloat16),
        ctx_grad,
        lengths_here,
    )
    col_span = key_full.shape[0] // model_groups
    pieces_out = []
    for group_idx in range(model_groups):
        key_part = key_full[group_idx * col_span : (group_idx + 1) * col_span]
        value_part = value_full[group_idx * col_span : (group_idx + 1) * col_span]
        partial_value = lax.dot_general(
            key_grad, key_part, (((1,), (1,)), ((), ())), preferred_element_type=jnp.float32
        )
        partial_value = partial_value + lax.dot_general(
            value_grad, value_part, (((1,), (1,)), ((), ())), preferred_element_type=jnp.float32
        )
        pieces_out.append(partial_value.astype(jnp.bfloat16))
    summed = lax.psum_scatter(
        jnp.concatenate(pieces_out, axis=1), "mp", scatter_dimension=1, tiled=True
    )
    outgoing_grad = through(recv_map.T, summed.reshape(block_count, -1), (peer_count, slot_count))
    returned = lax.all_to_all(outgoing_grad, "dp", split_axis=0, concat_axis=0, tiled=True)
    enc_grad = through(send_map.T, returned.reshape(all_slots, -1), (block_count,)).reshape(
        row_count, feature_width
    )
    return (context, enc_grad)


PAIR = 2 * DH


def nt(a, b):
    return lax.dot_general(a, b, (((1,), (1,)), ((), ())), preferred_element_type=F32)


def tn(a, b):
    return lax.dot_general(a, b, (((0,), (0,)), ((), ())), preferred_element_type=F32)


def forward_kernel(blocks, tab, x_ref, w_ref, q_ref, g_ref, ctx_ref, dkv_ref, acc, kv):
    step = pl.program_id(0)
    last = pl.num_programs(0) - 1
    part = jnp.dot(x_ref[...], w_ref[...], preferred_element_type=F32)

    @pl.when(step == 0)
    def _():
        acc[...] = part

    @pl.when((step > 0) & (step < last))
    def _():
        acc[...] += part

    @pl.when(step == last)
    def _():
        kv[...] = (acc[...] + part).astype(BF16)
        lane = lax.broadcasted_iota(jnp.int32, (BLOCK, PAIR), 1) < DH
        key_pos = lax.broadcasted_iota(jnp.int32, (BLOCK, PAIR), 0)
        scale = DH ** (-0.5)
        zero = jnp.zeros((BLOCK, PAIR), BF16)

        def one(b):
            src = tab[b]
            rows = pl.ds(pl.multiple_of(src * BLOCK, BLOCK), BLOCK)
            here = pl.ds(b * BLOCK, BLOCK)
            key = kv[rows, 0:PAIR]
            value = kv[rows, PAIR : 2 * PAIR]
            query = q_ref[here, :]
            grad = g_ref[here, :]
            query2 = jnp.concatenate(
                [jnp.where(lane, query, zero), jnp.where(lane, zero, query)], axis=0
            )
            grad2 = jnp.concatenate(
                [jnp.where(lane, grad, zero), jnp.where(lane, zero, grad)], axis=0
            )
            scores = jnp.where(key_pos < tab[blocks + b], nt(key, query2) * scale, -1e30)
            weights = jnp.exp(scores - jnp.max(scores, axis=0, keepdims=True))
            probs = weights / jnp.sum(weights, axis=0, keepdims=True)
            prob_bf = probs.astype(BF16)
            ctx2 = tn(prob_bf, value)
            ctx_ref[here, :] = jnp.where(lane, ctx2[:BLOCK], ctx2[BLOCK:]).astype(BF16)
            prob_grad = nt(value, grad2)
            row_dot = jnp.sum(probs * prob_grad, axis=0, keepdims=True)
            score_grad = (probs * (prob_grad - row_dot) * scale).astype(BF16)
            dkv_ref[rows, 0:PAIR] = jnp.dot(
                score_grad, query2, preferred_element_type=F32
            ).astype(BF16)
            dkv_ref[rows, PAIR : 2 * PAIR] = jnp.dot(
                prob_bf, grad2, preferred_element_type=F32
            ).astype(BF16)

        for b in range(blocks):
            one(b)


def forward_chunk(table, x, w, queries, grads, chunk, blocks, parts):
    rows, width = x.shape
    cols = w.shape[1]
    span = width // parts
    return pl.pallas_call(
        functools.partial(forward_kernel, blocks),
        grid_spec=pltpu.PrefetchScalarGridSpec(
            num_scalar_prefetch=1,
            grid=(parts,),
            in_specs=[
                pl.BlockSpec((rows, span), lambda a, t: (0, t[2 * blocks + a])),
                pl.BlockSpec((span, cols), lambda a, t: (a, 0)),
                pl.BlockSpec((rows, PAIR), lambda a, t: (0, chunk)),
                pl.BlockSpec((rows, PAIR), lambda a, t: (0, chunk)),
            ],
            out_specs=[
                pl.BlockSpec((rows, PAIR), lambda a, t: (0, 0)),
                pl.BlockSpec((rows, 2 * PAIR), lambda a, t: (0, 0)),
            ],
            scratch_shapes=[
                pltpu.VMEM((rows, cols), F32),
                pltpu.VMEM((rows, cols), BF16),
            ],
        ),
        out_shape=[
            jax.ShapeDtypeStruct((rows, PAIR), BF16),
            jax.ShapeDtypeStruct((rows, 2 * PAIR), BF16),
        ],
        compiler_params=pltpu.CompilerParams(vmem_limit_bytes=32 << 20),
        cost_estimate=pl.CostEstimate(
            flops=2 * rows * width * cols + 10 * rows * BLOCK * 2 * PAIR,
            bytes_accessed=2 * rows * width + 2 * width * cols + 6 * rows * PAIR * 2,
            transcendentals=rows * BLOCK * 2,
        ),
        name="fwd",
    )(table, x, w, queries, grads)


def backward_kernel(has_acc, tab, dkv_ref, w_ref, *refs):
    out_ref = refs[-1]
    part = nt(dkv_ref[...], w_ref[...])
    if has_acc:
        part = part + refs[0][...]
    out_ref[...] = part.astype(out_ref.dtype)


def backward_chunk(table, dkv, w, acc, blocks, parts, row_at, row_n, out_dtype, alias):
    rows, cols = dkv.shape
    width = w.shape[0]
    span = width // parts
    tile = min(row_n, 512)
    first = row_at // tile
    in_specs = [
        pl.BlockSpec((tile, cols), lambda r, a, t: (first + r, 0)),
        pl.BlockSpec((span, cols), lambda r, a, t: (a, 0)),
    ]
    operands = [table, dkv, w]
    if acc is not None:
        in_specs.append(
            pl.BlockSpec((tile, span), lambda r, a, t: (first + r, t[2 * blocks + a]))
        )
        operands.append(acc)
    return pl.pallas_call(
        functools.partial(backward_kernel, acc is not None),
        grid_spec=pltpu.PrefetchScalarGridSpec(
            num_scalar_prefetch=1,
            grid=(row_n // tile, parts),
            in_specs=in_specs,
            out_specs=pl.BlockSpec((tile, span), lambda r, a, t: (r, t[2 * blocks + a])),
        ),
        out_shape=jax.ShapeDtypeStruct((row_n, width), out_dtype),
        input_output_aliases={3: 0} if alias else {},
        compiler_params=pltpu.CompilerParams(vmem_limit_bytes=32 << 20),
        cost_estimate=pl.CostEstimate(
            flops=2 * row_n * width * cols,
            bytes_accessed=2 * row_n * cols + 2 * width * cols + 8 * row_n * width,
            transcendentals=0,
        ),
        name="bwd",
    )(*operands)


def shards_section(enc_rows, enc_len, dest_dp, peer_counts, queries, ctx_grad, w_key, w_value):
    n_sec, n_dp, n_mp = (lax.axis_size(a) for a in ("section", "dp", "mp"))
    z, d, m = (lax.axis_index(a) for a in ("section", "dp", "mp"))
    own_blocks = dest_dp.shape[0]
    blocks = own_blocks * n_dp
    own_rows, half = enc_rows.shape
    head_cols = w_key.shape[1] // n_dp
    chunks = head_cols // PAIR

    core = [(i, i ^ 1) for i in range(n_dp)]
    ypairs = [(i, i ^ 2) for i in range(n_dp)]
    xpairs = [(0, 1), (1, 0)]
    up = [(i, i + 1) for i in range(n_sec - 1)]
    down = [(i + 1, i) for i in range(n_sec - 1)]
    over_two = [(i, i ^ 2) for i in range(n_sec)]
    ends = [(1, 0), (2, 3)]

    packed = jnp.concatenate([enc_len, dest_dp, peer_counts[0]])
    packed = lax.all_gather(packed, "dp", axis=0, tiled=False)
    lens = packed[:, :own_blocks].reshape(-1)
    dest = packed[:, own_blocks : 2 * own_blocks]
    counts = packed[:, 2 * own_blocks :]
    pos = jnp.arange(own_blocks, dtype=jnp.int32)
    peer = jnp.arange(n_dp, dtype=jnp.int32)
    counts_before = jnp.sum(
        jnp.where(peer[None, None, :] < peer[None, :, None], counts[:, None, :], 0), axis=2
    )
    ends_at = counts_before + counts
    sender = jnp.sum((ends_at[:, None, :] <= pos[None, :, None]).astype(jnp.int32), axis=2)
    is_sender = sender[:, :, None] == peer[None, None, :]
    rank = pos[None, :] - jnp.sum(jnp.where(is_sender, counts_before[:, None, :], 0), axis=2)
    same = dest[:, :, None] == dest[:, None, :]
    slot_rank = jnp.sum((same & (pos[None, None, :] < pos[None, :, None])).astype(jnp.int32), axis=2)
    hit = (
        is_sender[:, :, :, None]
        & (dest[None, None] == peer[:, None, None, None])
        & (slot_rank[None, None] == rank[:, :, None, None])
    ).reshape(blocks, blocks)
    near = peer ^ d
    slot = jnp.where(near == 1, 2, jnp.where(near == 2, 1, near))
    place = (slot[:, None] * own_blocks + pos[None, :]).reshape(-1)
    src = jnp.sum(jnp.where(hit, place[None, :], 0), axis=1)
    src_len = jnp.sum(jnp.where(hit, lens[None, :], 0), axis=1)
    sec_at = (z + jnp.arange(n_sec, dtype=jnp.int32)) % n_sec
    sec_half = n_sec // n_mp
    col_at = ((sec_at // sec_half) ^ m) * sec_half + sec_at % sec_half
    table = jnp.concatenate([src, src_len, col_at]).astype(jnp.int32)

    def weight_chunk(c):
        def cut(w):
            return w.reshape(own_rows, n_dp, head_cols)[:, :, c * PAIR : (c + 1) * PAIR]

        both = jnp.concatenate([cut(w_key), cut(w_value)], axis=2).transpose(1, 0, 2)
        got = lax.all_to_all(both, "dp", split_axis=0, concat_axis=0, tiled=True)
        return got.reshape(n_dp * own_rows, 2 * PAIR)

    own = [weight_chunk(c) for c in range(chunks)]

    e_y = lax.ppermute(enc_rows, "dp", ypairs)
    e_x = lax.ppermute(enc_rows, "mp", xpairs)
    e_yx = lax.ppermute(e_y, "mp", xpairs)
    top = jnp.concatenate(
        [jnp.concatenate([enc_rows, e_x], axis=1), jnp.concatenate([e_y, e_yx], axis=1)], axis=0
    )
    x = jnp.concatenate([top, lax.ppermute(top, "dp", core)], axis=0)

    def to_heads(rows):
        parts = rows.reshape(own_rows, n_dp, head_cols).transpose(1, 0, 2)
        got = lax.all_to_all(parts, "dp", split_axis=0, concat_axis=0, tiled=True)
        return got.reshape(n_dp * own_rows, head_cols)

    q_all = to_heads(queries)
    g_all = to_heads(ctx_grad)

    acc = None
    contexts = []
    gate = None
    for c in range(chunks):
        piece = own[c]
        if gate is not None:
            piece, _ = lax.optimization_barrier((piece, gate))
        below = lax.ppermute(piece, "section", up)
        above = lax.ppermute(piece, "section", down)
        far = lax.ppermute(piece, "section", over_two)
        end = lax.ppermute(far, "section", ends)
        gate = far
        w = jnp.concatenate(
            [
                own[c],
                jnp.where(z == n_sec - 1, end, above),
                far,
                jnp.where(z == 0, end, below),
            ],
            axis=0,
        )
        ctx, dkv = forward_chunk(table, x, w, q_all, g_all, c, blocks, n_sec)
        ctx4 = ctx.reshape(n_dp, own_rows, PAIR)
        contexts.append(lax.all_to_all(ctx4, "dp", split_axis=0, concat_axis=0, tiled=True))
        back = functools.partial(backward_chunk, table, dkv, w, acc, blocks, n_sec)
        rows = x.shape[0]
        if c < chunks - 1:
            acc = back(0, rows, F32, acc is not None)
        else:
            give = back(rows // 2, rows // 2, BF16, False)
            keep = back(0, rows // 2, F32, False)

    context = jnp.stack(contexts, axis=2)
    context = context.transpose(1, 0, 2, 3).reshape(own_rows, n_dp * head_cols)

    keep = keep + lax.ppermute(give, "dp", core).astype(F32)
    q4 = half // 2

    def cols(a, lo):
        return a[:, lo : lo + q4]

    p_y = jnp.concatenate([cols(keep[own_rows:], 0), cols(keep[own_rows:], half)], axis=1)
    q_x = cols(keep, half + q4)
    got_y = lax.ppermute(p_y.astype(BF16), "dp", ypairs).astype(F32)
    got_x = lax.ppermute(q_x.astype(BF16), "mp", xpairs).astype(F32)
    p_own = cols(keep[:own_rows], 0) + got_y[:, :q4]
    p_x = cols(keep[:own_rows], half) + got_y[:, q4:]
    q_own = cols(keep, q4) + got_x
    p_own = p_own + lax.ppermute(p_x.astype(BF16), "mp", xpairs).astype(F32)
    q_fin = q_own[:own_rows] + lax.ppermute(
        q_own[own_rows:].astype(BF16), "dp", ypairs
    ).astype(F32)
    enc_grad = jnp.concatenate([p_own.astype(BF16), q_fin.astype(BF16)], axis=1)
    return (context, enc_grad)


def solution(mesh):
    placed = (
        P(("section", "dp"), "mp"),
        P(("section", "dp")),
        P(("section", "dp")),
        P(("section", "dp"), None),
        P(("section", "dp"), "mp"),
        P(("section", "dp"), "mp"),
        P(("section", "dp"), "mp"),
        P(("section", "dp"), "mp"),
    )
    sizes = tuple(mesh.shape[a] for a in ("section", "dp", "mp"))
    body = shards_section if sizes == (4, 4, 2) else shards_general
    return jax.shard_map(
        body,
        mesh=mesh,
        in_specs=placed,
        out_specs=(P(("section", "dp"), "mp"), P(("section", "dp"), "mp")),
        check_vma=False,
    )
```

```python
import functools

import jax
import jax.numpy as jnp
from jax import lax
from jax.experimental import pallas as pl
from jax.experimental.pallas import tpu as pltpu
from jax.sharding import PartitionSpec as P

DH = 64
BLOCK = 64
F32 = jnp.float32
BF16 = jnp.bfloat16


def attend(query_rows, key_rows, value_rows, grad_rows, key_lengths):
    block_count = key_lengths.shape[0]
    head_count = query_rows.shape[1] // DH
    shape_four = (block_count, BLOCK, head_count, DH)
    query_heads = query_rows.reshape(shape_four)
    key_heads = key_rows.reshape(shape_four)
    value_heads = value_rows.reshape(shape_four)
    grad_heads = grad_rows.reshape(shape_four)
    score_scale = DH ** (-0.5)
    scores = (
        jnp.einsum("bihd,bjhd->bhij", query_heads, key_heads, preferred_element_type=jnp.float32)
        * score_scale
    )
    visible = (
        jnp.arange(BLOCK, dtype=jnp.float32)[None, None, None, :] < key_lengths[:, None, None, None]
    )
    scores = jnp.where(visible, scores, -1e30)
    row_max = jnp.max(scores, axis=-1, keepdims=True)
    weights_exp = jnp.exp(scores - row_max)
    probabilities = weights_exp / jnp.sum(weights_exp, axis=-1, keepdims=True)
    prob_bf = probabilities.astype(jnp.bfloat16)
    context = jnp.einsum(
        "bhij,bjhd->bihd", prob_bf, value_heads, preferred_element_type=jnp.float32
    ).astype(jnp.bfloat16)
    prob_grad = jnp.einsum(
        "bihd,bjhd->bhij", grad_heads, value_heads, preferred_element_type=jnp.float32
    )
    row_dot = jnp.sum(probabilities * prob_grad, axis=-1, keepdims=True)
    score_grad = (probabilities * (prob_grad - row_dot) * score_scale).astype(jnp.bfloat16)
    key_grad = jnp.einsum(
        "bhij,bihd->bjhd", score_grad, query_heads, preferred_element_type=jnp.float32
    ).astype(jnp.bfloat16)
    value_grad = jnp.einsum(
        "bhij,bihd->bjhd", prob_bf, grad_heads, preferred_element_type=jnp.float32
    ).astype(jnp.bfloat16)
    flat_shape = (block_count * BLOCK, head_count * DH)
    return (
        context.reshape(flat_shape),
        key_grad.reshape(flat_shape),
        value_grad.reshape(flat_shape),
    )


def through(table, data, lead_shape):
    moved = jnp.dot(table, data, preferred_element_type=jnp.float32).astype(jnp.bfloat16)
    return moved.reshape(lead_shape + data.shape[1:])


def shards_general(enc_rows, enc_len, dest_dp, peer_counts, queries, ctx_grad, w_key, w_value):
    peer_count = lax.axis_size("dp")
    model_groups = lax.axis_size("mp")
    block_count = dest_dp.shape[0]
    slot_count = max(2, -(-block_count // peer_count))
    row_count, feature_width = enc_rows.shape
    key_full, value_full = (
        lax.all_gather(w_key, ("section", "dp"), axis=0, tiled=True),
        lax.all_gather(w_value, ("section", "dp"), axis=0, tiled=True),
    )
    positions = jnp.arange(block_count, dtype=jnp.int32)
    same_dest = dest_dp[:, None] == dest_dp[None, :]
    slot_rank = jnp.sum(
        (same_dest & (positions[None, :] < positions[:, None])).astype(jnp.int32), axis=1
    )
    target_slot = dest_dp * slot_count + slot_rank
    slot_ids = jnp.arange(peer_count * slot_count, dtype=jnp.int32)
    send_map = (slot_ids[:, None] == target_slot[None, :]).astype(jnp.bfloat16)
    arrivals = peer_counts[0]
    arrival_ends = jnp.cumsum(arrivals)
    sender = jnp.sum((arrival_ends[None, :] <= positions[:, None]).astype(jnp.int32), axis=1)
    first_pos = jnp.take(arrival_ends, sender) - jnp.take(arrivals, sender)
    slot_pick = sender * slot_count + positions - first_pos
    recv_map = (slot_pick[:, None] == slot_ids[None, :]).astype(jnp.bfloat16)
    lengths_own = enc_len.astype(jnp.float32).astype(jnp.bfloat16).reshape(block_count, 1)
    all_slots = peer_count * slot_count
    outgoing = through(send_map, enc_rows.reshape(block_count, -1), (peer_count, slot_count))
    outgoing_len = through(send_map, lengths_own, (peer_count, slot_count))
    incoming, incoming_len = (
        lax.all_to_all(outgoing, "dp", split_axis=0, concat_axis=0, tiled=True),
        lax.all_to_all(outgoing_len, "dp", split_axis=0, concat_axis=0, tiled=True),
    )
    rows_here = through(recv_map, incoming.reshape(all_slots, -1), (block_count,)).reshape(
        row_count, feature_width
    )
    lengths_here = through(recv_map, incoming_len.reshape(all_slots, 1), (block_count,))[
        :, 0
    ].astype(jnp.float32)
    shard_cols = lax.all_gather(rows_here, "mp", axis=1, tiled=True)
    key_acc = jnp.dot(shard_cols, key_full, preferred_element_type=jnp.float32)
    value_acc = jnp.dot(shard_cols, value_full, preferred_element_type=jnp.float32)
    context, key_grad, value_grad = attend(
        queries,
        key_acc.astype(jnp.bfloat16),
        value_acc.astype(jnp.bfloat16),
        ctx_grad,
        lengths_here,
    )
    col_span = key_full.shape[0] // model_groups
    pieces_out = []
    for group_idx in range(model_groups):
        key_part = key_full[group_idx * col_span : (group_idx + 1) * col_span]
        value_part = value_full[group_idx * col_span : (group_idx + 1) * col_span]
        partial_value = lax.dot_general(
            key_grad, key_part, (((1,), (1,)), ((), ())), preferred_element_type=jnp.float32
        )
        partial_value = partial_value + lax.dot_general(
            value_grad, value_part, (((1,), (1,)), ((), ())), preferred_element_type=jnp.float32
        )
        pieces_out.append(partial_value.astype(jnp.bfloat16))
    summed = lax.psum_scatter(
        jnp.concatenate(pieces_out, axis=1), "mp", scatter_dimension=1, tiled=True
    )
    outgoing_grad = through(recv_map.T, summed.reshape(block_count, -1), (peer_count, slot_count))
    returned = lax.all_to_all(outgoing_grad, "dp", split_axis=0, concat_axis=0, tiled=True)
    enc_grad = through(send_map.T, returned.reshape(all_slots, -1), (block_count,)).reshape(
        row_count, feature_width
    )
    return (context, enc_grad)


PAIR = 2 * DH


def nt(a, b):
    return lax.dot_general(a, b, (((1,), (1,)), ((), ())), preferred_element_type=F32)


def tn(a, b):
    return lax.dot_general(a, b, (((0,), (0,)), ((), ())), preferred_element_type=F32)


def after(value, *needed):
    return lax.optimization_barrier((value,) + needed)[0]


def forward_kernel(n_dp, n_sec, n_half, blk, tab, *refs):
    blocks = n_dp * blk
    x_refs = refs[: n_half * n_dp]
    refs = refs[n_half * n_dp :]
    own, above, far, below, end = refs[:5]
    q_refs = refs[5 : 5 + n_dp]
    g_refs = refs[5 + n_dp : 5 + 2 * n_dp]
    refs = refs[5 + 2 * n_dp :]
    ctx_refs = refs[:n_dp]
    dkv_ref, w_ref, acc, kv = refs[n_dp:]
    rows = own.shape[0] // n_dp
    step = pl.program_id(0)
    z = tab[2 * blocks]
    d = tab[2 * blocks + 1]
    m = tab[2 * blocks + 2]
    per_half = n_sec // n_half
    section = (m ^ (step // per_half)) * per_half + step % per_half
    hop = (section - z + n_sec) % n_sec

    def take(ref):
        for t in range(n_dp):
            to = pl.multiple_of((d ^ t) * rows, rows)
            w_ref[pl.ds(to, rows), :] = ref[t * rows : (t + 1) * rows, :]

    @pl.when(hop == 0)
    def _():
        take(own)

    @pl.when((hop == 1) & (z != n_sec - 1))
    def _():
        take(above)

    @pl.when(hop == 2)
    def _():
        take(far)

    @pl.when((hop == n_sec - 1) & (z != 0))
    def _():
        take(below)

    @pl.when(((hop == 1) & (z == n_sec - 1)) | ((hop == n_sec - 1) & (z == 0)))
    def _():
        take(end)

    for h in range(n_half):

        @pl.when(step // per_half == h)
        def _():
            for t in range(n_dp):
                at = slice(t * rows, (t + 1) * rows)
                part = jnp.dot(
                    x_refs[h * n_dp + t][...], w_ref[...], preferred_element_type=F32
                )
                if h == 0:
                    acc[at, :] = jnp.where(step == 0, part, acc[at, :] + part)
                else:
                    acc[at, :] += part

    @pl.when(step == n_sec - 1)
    def _():
        kv[...] = acc[...].astype(BF16)
        lane = lax.broadcasted_iota(jnp.int32, (BLOCK, PAIR), 1) < DH
        key_pos = lax.broadcasted_iota(jnp.int32, (BLOCK, PAIR), 0)
        scale = DH ** (-0.5)
        zero = jnp.zeros((BLOCK, PAIR), BF16)

        def one(b):
            src = tab[b]
            source = pl.ds(pl.multiple_of(src * BLOCK, BLOCK), BLOCK)
            here = pl.ds((b % blk) * BLOCK, BLOCK)
            key = kv[source, 0:PAIR]
            value = kv[source, PAIR : 2 * PAIR]
            query = q_refs[b // blk][here, :]
            grad = g_refs[b // blk][here, :]
            query2 = jnp.concatenate(
                [jnp.where(lane, query, zero), jnp.where(lane, zero, query)], axis=0
            )
            grad2 = jnp.concatenate(
                [jnp.where(lane, grad, zero), jnp.where(lane, zero, grad)], axis=0
            )
            scores = jnp.where(key_pos < tab[blocks + b], nt(key, query2) * scale, -1e30)
            weights = jnp.exp(scores - jnp.max(scores, axis=0, keepdims=True))
            probs = weights / jnp.sum(weights, axis=0, keepdims=True)
            prob_bf = probs.astype(BF16)
            ctx2 = tn(prob_bf, value)
            ctx_refs[b // blk][here, :] = jnp.where(lane, ctx2[:BLOCK], ctx2[BLOCK:]).astype(BF16)
            prob_grad = nt(value, grad2)
            row_dot = jnp.sum(probs * prob_grad, axis=0, keepdims=True)
            score_grad = (probs * (prob_grad - row_dot) * scale).astype(BF16)
            dkv_ref[source, 0:PAIR] = jnp.dot(
                score_grad, query2, preferred_element_type=F32
            ).astype(BF16)
            dkv_ref[source, PAIR : 2 * PAIR] = jnp.dot(
                prob_bf, grad2, preferred_element_type=F32
            ).astype(BF16)

        for b in range(blocks):
            one(b)


def forward_chunk(table, x_pieces, pieces, q_own, g_own, qg, chunk, chunks, blk, n_sec):
    n_half = len(x_pieces)
    n_dp = len(x_pieces[0])
    rows, half = x_pieces[0][0].shape
    per_half = n_sec // n_half
    span = half // per_half
    cols = 2 * PAIR
    blocks = n_dp * blk

    def x_spec(h):
        def at(a, t):
            return (0, jnp.clip(a - h * per_half, 0, per_half - 1))

        return pl.BlockSpec((rows, span), at)

    whole = pl.BlockSpec((span, cols), lambda a, t: (0, 0))
    mine = pl.BlockSpec((rows, PAIR), lambda a, t: (0, t[2 * blocks + 1] * chunks + chunk))

    def head(at):
        return pl.BlockSpec((rows, PAIR), lambda a, t: (0, at))

    return pl.pallas_call(
        functools.partial(forward_kernel, n_dp, n_sec, n_half, blk),
        grid_spec=pltpu.PrefetchScalarGridSpec(
            num_scalar_prefetch=1,
            grid=(n_sec,),
            in_specs=[x_spec(h) for h in range(n_half) for _ in range(n_dp)]
            + [whole] * 5
            + [mine]
            + [head(chunk)] * (n_dp - 1)
            + [mine]
            + [head(chunks + chunk)] * (n_dp - 1),
            out_specs=[pl.BlockSpec((rows, PAIR), lambda a, t: (0, 0))] * n_dp
            + [
                pl.BlockSpec((n_dp * rows, cols), lambda a, t: (0, 0)),
                pl.BlockSpec((span, cols), lambda a, t: (a, 0)),
            ],
            scratch_shapes=[
                pltpu.VMEM((n_dp * rows, cols), F32),
                pltpu.VMEM((n_dp * rows, cols), BF16),
            ],
        ),
        out_shape=[jax.ShapeDtypeStruct((rows, PAIR), BF16)] * n_dp
        + [
            jax.ShapeDtypeStruct((n_dp * rows, cols), BF16),
            jax.ShapeDtypeStruct((n_sec * span, cols), BF16),
        ],
        compiler_params=pltpu.CompilerParams(vmem_limit_bytes=40 << 20),
        cost_estimate=pl.CostEstimate(
            flops=2 * n_dp * rows * n_sec * span * cols,
            bytes_accessed=2 * n_dp * rows * n_sec * span + 4 * n_sec * span * cols,
            transcendentals=n_dp * rows * BLOCK * 2,
        ),
        name="fwd",
    )(
        table,
        *[piece for halves in x_pieces for piece in halves],
        *pieces,
        q_own,
        *qg,
        g_own,
        *qg,
    )


def give_kernel(chunks, *refs):
    total = nt(refs[0][...], refs[chunks][...])
    for c in range(1, chunks):
        total += nt(refs[c][...], refs[chunks + c][...])
    refs[-1][...] = total.astype(BF16)


def keep_kernel(chunks, y_first, *refs):
    half, row = pl.program_id(0), pl.program_id(1)
    total = refs[2 * chunks][...].astype(F32)
    for c in range(chunks):
        total += nt(refs[c][...], refs[chunks + c][...])
    if y_first:
        own_ref, x_ref, y_ref = refs[2 * chunks + 1 :]

        @pl.when((half == 0) & (row == 0))
        def _():
            own_ref[...] = total

        @pl.when((half == 1) & (row == 0))
        def _():
            x_ref[...] = total

        @pl.when(row == 1)
        def _():
            y_ref[...] = total.astype(BF16)
    else:
        own_ref, x_ref = refs[2 * chunks + 1 :]

        @pl.when(half == 0)
        def _():
            own_ref[...] = total

        @pl.when(half == 1)
        def _():
            x_ref[...] = total.astype(BF16)


def backward(dkvs, ws, received, part, rows, per_half, y_first):
    chunks = len(dkvs)
    cols = dkvs[0].shape[1]
    span = ws[0].shape[0] // (2 * per_half)
    which = 1 if received is None else 0
    specs = [pl.BlockSpec((rows, cols), lambda h, r: (2 * r + which, 0))] * chunks
    specs += [pl.BlockSpec((span, cols), lambda h, r: (h * per_half + part, 0))] * chunks
    block = pl.BlockSpec((rows, span), lambda h, r: (r, h))
    fixed = pl.BlockSpec((rows, span), lambda h, r: (0, 0))
    if received is None:
        kernel = functools.partial(give_kernel, chunks)
        out_specs, out_shape = block, jax.ShapeDtypeStruct((2 * rows, 2 * span), BF16)
        extra = ()
    else:
        kernel = functools.partial(keep_kernel, chunks, y_first)
        specs = specs + [block]
        extra = (received,)
        if y_first:
            out_specs = [fixed, fixed, pl.BlockSpec((rows, span), lambda h, r: (0, h))]
            out_shape = [
                jax.ShapeDtypeStruct((rows, span), F32),
                jax.ShapeDtypeStruct((rows, span), F32),
                jax.ShapeDtypeStruct((rows, 2 * span), BF16),
            ]
        else:
            out_specs = [
                pl.BlockSpec((rows, span), lambda h, r: (jnp.where(h == 0, r, 1), 0)),
                pl.BlockSpec((rows, span), lambda h, r: (jnp.where(h == 1, r, 0), 0)),
            ]
            out_shape = [
                jax.ShapeDtypeStruct((2 * rows, span), F32),
                jax.ShapeDtypeStruct((2 * rows, span), BF16),
            ]
    return pl.pallas_call(
        kernel,
        grid=(2, 2),
        in_specs=specs,
        out_specs=out_specs,
        out_shape=out_shape,
        compiler_params=pltpu.CompilerParams(vmem_limit_bytes=32 << 20),
        cost_estimate=pl.CostEstimate(
            flops=8 * rows * span * cols * chunks,
            bytes_accessed=4 * span * cols * chunks + 16 * rows * span,
            transcendentals=0,
        ),
        name="bwd",
    )(*dkvs, *ws, *extra)


def context_kernel(n_dp, chunks, tab, *refs):
    out = refs[-1]
    for t in range(n_dp):
        for c in range(chunks):
            at = (tab[0] ^ t) * (chunks * PAIR) + c * PAIR
            out[:, pl.ds(pl.multiple_of(at, PAIR), PAIR)] = refs[t * chunks + c][...]


def gather_context(d, parts):
    n_dp, chunks = len(parts), len(parts[0])
    rows = parts[0][0].shape[0]
    vmem = pl.BlockSpec(memory_space=pltpu.VMEM)
    return pl.pallas_call(
        functools.partial(context_kernel, n_dp, chunks),
        in_specs=[pl.BlockSpec(memory_space=pltpu.SMEM)] + [vmem] * (n_dp * chunks),
        out_specs=vmem,
        out_shape=jax.ShapeDtypeStruct((rows, n_dp * chunks * PAIR), BF16),
        name="gather_context",
    )(d.reshape(1), *[piece for row in parts for piece in row])


def shards_section(enc_rows, enc_len, dest_dp, peer_counts, queries, ctx_grad, w_key, w_value):
    n_sec, n_dp, n_mp = (lax.axis_size(a) for a in ("section", "dp", "mp"))
    z, d, m = (lax.axis_index(a).astype(jnp.int32) for a in ("section", "dp", "mp"))
    blk = dest_dp.shape[0]
    blocks = blk * n_dp
    rows, half = enc_rows.shape
    head_cols = w_key.shape[1] // n_dp
    chunks = head_cols // PAIR

    near = [[(i, i ^ t) for i in range(n_dp)] for t in range(n_dp)]
    xpairs = [(0, 1), (1, 0)]
    up = [(i, i + 1) for i in range(n_sec - 1)]
    down = [(i + 1, i) for i in range(n_sec - 1)]
    over_two = [(i, i ^ 2) for i in range(n_sec)]
    ends = [(1, 0), (2, 3)]

    def weight_chunk(c, *needed):
        w_k, w_v = w_key, w_value
        if needed:
            w_k, w_v = lax.optimization_barrier((w_key, w_value) + needed)[:2]
        got = []
        for t in range(n_dp):
            at = (d ^ t) * head_cols + c * PAIR
            cut = jnp.concatenate(
                [lax.dynamic_slice(w, (0, at), (rows, PAIR)) for w in (w_k, w_v)], axis=1
            )
            got.append(cut if t == 0 else lax.ppermute(cut, "dp", near[t]))
        return jnp.concatenate(got, axis=0)

    own = [weight_chunk(0)]

    packed = jnp.concatenate([enc_len, dest_dp, peer_counts[0]]).reshape(1, -1)
    packs = jnp.concatenate(
        [packed] + [lax.ppermute(packed, "dp", near[t]) for t in range(1, n_dp)], axis=0
    )
    peer = jnp.arange(n_dp, dtype=jnp.int32)
    order = (peer[:, None] ^ d) == peer[None, :]
    packs = jnp.sum(jnp.where(order[:, :, None], packs[None], 0), axis=1)
    lens = packs[:, :blk].reshape(-1)
    dest = packs[:, blk : 2 * blk]
    counts = packs[:, 2 * blk :]
    pos = jnp.arange(blk, dtype=jnp.int32)
    before = jnp.sum(
        jnp.where(peer[None, None, :] < peer[None, :, None], counts[:, None, :], 0), axis=2
    )
    upto = before + counts
    sender = jnp.sum((upto[:, None, :] <= pos[None, :, None]).astype(jnp.int32), axis=2)
    is_sender = sender[:, :, None] == peer[None, None, :]
    rank = pos[None, :] - jnp.sum(jnp.where(is_sender, before[:, None, :], 0), axis=2)
    same = dest[:, :, None] == dest[:, None, :]
    slot_rank = jnp.sum((same & (pos[None, None, :] < pos[None, :, None])).astype(jnp.int32), axis=2)
    hit = (
        is_sender[:, :, :, None]
        & (dest[None, None] == peer[:, None, None, None])
        & (slot_rank[None, None] == rank[:, :, None, None])
    ).reshape(n_dp, blk, blocks)
    place = ((peer ^ d)[:, None] * blk + pos[None, :]).reshape(-1)
    src = jnp.sum(jnp.where(hit, place, 0), axis=2)
    src_len = jnp.sum(jnp.where(hit, lens, 0), axis=2)
    both = jnp.stack([src, src_len])
    both = jnp.sum(jnp.where(order[None, :, :, None], both[:, None], 0), axis=2)
    table = jnp.concatenate([both.reshape(-1), jnp.stack([z, d, m])])

    e_x = lax.ppermute(enc_rows, "mp", xpairs)
    e_y = lax.ppermute(after(enc_rows, own[0]), "dp", near[2])
    e_yx = lax.ppermute(e_y, "mp", xpairs)
    x_pieces = []
    for a, b in ((enc_rows, e_y), (e_x, e_yx)):
        x_pieces.append((a, lax.ppermute(a, "dp", near[1]), b, lax.ppermute(b, "dp", near[1])))

    own.append(weight_chunk(1, own[0]))

    q_in, g_in = lax.optimization_barrier((queries, ctx_grad, e_y))[:2]
    qg = []
    for t in range(1, n_dp):
        cut = jnp.concatenate(
            [
                lax.dynamic_slice(a, (0, (d ^ t) * head_cols), (rows, head_cols))
                for a in (q_in, g_in)
            ],
            axis=1,
        )
        qg.append(lax.ppermute(cut, "dp", near[t]))
    for c in range(2, chunks):
        own.append(weight_chunk(c, qg[-1], own[-1]))

    dkvs, ws, contexts = [], [], [[] for _ in range(n_dp)]
    below, above, far, end = ([None] * chunks for _ in range(4))
    for c in range(chunks):
        piece, piece_far = own[c], own[c]
        if c > 0:
            needed = (below[c - 1], above[c - 1]) + tuple(dkvs[c - 3 : c - 2] if c > 2 else ())
            piece = after(piece, *needed)
            piece_far = after(piece_far, far[c - 1])
        below[c] = lax.ppermute(piece, "section", up)
        above[c] = lax.ppermute(piece, "section", down)
        far[c] = lax.ppermute(piece_far, "section", over_two)
        turn = far[c] if c < 3 else after(far[c], dkvs[c - 2])
        end[c] = lax.ppermute(turn, "section", ends)
        done = c - 1
        for k in ([done] if done >= 0 else []) + ([c] if c == chunks - 1 else []):
            out = forward_chunk(
                table,
                x_pieces,
                (own[k], above[k], far[k], below[k], end[k]),
                queries,
                ctx_grad,
                qg,
                k,
                chunks,
                blk,
                n_sec,
            )
            dkvs.append(out[n_dp])
            ws.append(out[n_dp + 1])
            contexts[0].append(out[0])
            for t in range(1, n_dp):
                contexts[t].append(lax.ppermute(out[t], "dp", near[t]))

    per_half = n_sec // n_mp
    back = functools.partial(backward, dkvs, ws, rows=rows, per_half=per_half)
    give_p = lax.ppermute(back(None, part=0, y_first=True), "dp", near[1])
    give_q = lax.ppermute(back(None, part=1, y_first=False), "dp", near[1])
    p_own, p_x, p_y = back(give_p, part=0, y_first=True)
    got_y = lax.ppermute(p_y, "dp", near[2]).astype(F32)
    q_own, q_x = back(give_q, part=1, y_first=False)
    got_x = lax.ppermute(q_x, "mp", xpairs).astype(F32)
    span = p_own.shape[1]
    last_x = lax.ppermute((p_x + got_y[:, span:]).astype(BF16), "mp", xpairs).astype(F32)
    last_y = lax.ppermute((q_own[rows:] + got_x[rows:]).astype(BF16), "dp", near[2]).astype(F32)
    enc_grad = jnp.concatenate(
        [
            (p_own + got_y[:, :span] + last_x).astype(BF16),
            (q_own[:rows] + got_x[:rows] + last_y).astype(BF16),
        ],
        axis=1,
    )
    return (gather_context(d, contexts), enc_grad)


def solution(mesh):
    placed = (
        P(("section", "dp"), "mp"),
        P(("section", "dp")),
        P(("section", "dp")),
        P(("section", "dp"), None),
        P(("section", "dp"), "mp"),
        P(("section", "dp"), "mp"),
        P(("section", "dp"), "mp"),
        P(("section", "dp"), "mp"),
    )
    sizes = tuple(mesh.shape[a] for a in ("section", "dp", "mp"))
    body = shards_section if sizes == (4, 4, 2) else shards_general
    return jax.shard_map(
        body,
        mesh=mesh,
        in_specs=placed,
        out_specs=(P(("section", "dp"), "mp"), P(("section", "dp"), "mp")),
        check_vma=False,
    )
```

```python
import functools

import jax
import jax.numpy as jnp
from jax import lax
from jax.experimental import pallas as pl
from jax.experimental.pallas import tpu as pltpu
from jax.sharding import PartitionSpec as P

DH = 64
BLOCK = 64
F32 = jnp.float32
BF16 = jnp.bfloat16


def attend(query_rows, key_rows, value_rows, grad_rows, key_lengths):
    block_count = key_lengths.shape[0]
    head_count = query_rows.shape[1] // DH
    shape_four = (block_count, BLOCK, head_count, DH)
    query_heads = query_rows.reshape(shape_four)
    key_heads = key_rows.reshape(shape_four)
    value_heads = value_rows.reshape(shape_four)
    grad_heads = grad_rows.reshape(shape_four)
    score_scale = DH ** (-0.5)
    scores = (
        jnp.einsum("bihd,bjhd->bhij", query_heads, key_heads, preferred_element_type=jnp.float32)
        * score_scale
    )
    visible = (
        jnp.arange(BLOCK, dtype=jnp.float32)[None, None, None, :] < key_lengths[:, None, None, None]
    )
    scores = jnp.where(visible, scores, -1e30)
    row_max = jnp.max(scores, axis=-1, keepdims=True)
    weights_exp = jnp.exp(scores - row_max)
    probabilities = weights_exp / jnp.sum(weights_exp, axis=-1, keepdims=True)
    prob_bf = probabilities.astype(jnp.bfloat16)
    context = jnp.einsum(
        "bhij,bjhd->bihd", prob_bf, value_heads, preferred_element_type=jnp.float32
    ).astype(jnp.bfloat16)
    prob_grad = jnp.einsum(
        "bihd,bjhd->bhij", grad_heads, value_heads, preferred_element_type=jnp.float32
    )
    row_dot = jnp.sum(probabilities * prob_grad, axis=-1, keepdims=True)
    score_grad = (probabilities * (prob_grad - row_dot) * score_scale).astype(jnp.bfloat16)
    key_grad = jnp.einsum(
        "bhij,bihd->bjhd", score_grad, query_heads, preferred_element_type=jnp.float32
    ).astype(jnp.bfloat16)
    value_grad = jnp.einsum(
        "bhij,bihd->bjhd", prob_bf, grad_heads, preferred_element_type=jnp.float32
    ).astype(jnp.bfloat16)
    flat_shape = (block_count * BLOCK, head_count * DH)
    return (
        context.reshape(flat_shape),
        key_grad.reshape(flat_shape),
        value_grad.reshape(flat_shape),
    )


def through(table, data, lead_shape):
    moved = jnp.dot(table, data, preferred_element_type=jnp.float32).astype(jnp.bfloat16)
    return moved.reshape(lead_shape + data.shape[1:])


def shards_general(enc_rows, enc_len, dest_dp, peer_counts, queries, ctx_grad, w_key, w_value):
    peer_count = lax.axis_size("dp")
    model_groups = lax.axis_size("mp")
    block_count = dest_dp.shape[0]
    slot_count = max(2, -(-block_count // peer_count))
    row_count, feature_width = enc_rows.shape
    key_full, value_full = (
        lax.all_gather(w_key, ("section", "dp"), axis=0, tiled=True),
        lax.all_gather(w_value, ("section", "dp"), axis=0, tiled=True),
    )
    positions = jnp.arange(block_count, dtype=jnp.int32)
    same_dest = dest_dp[:, None] == dest_dp[None, :]
    slot_rank = jnp.sum(
        (same_dest & (positions[None, :] < positions[:, None])).astype(jnp.int32), axis=1
    )
    target_slot = dest_dp * slot_count + slot_rank
    slot_ids = jnp.arange(peer_count * slot_count, dtype=jnp.int32)
    send_map = (slot_ids[:, None] == target_slot[None, :]).astype(jnp.bfloat16)
    arrivals = peer_counts[0]
    arrival_ends = jnp.cumsum(arrivals)
    sender = jnp.sum((arrival_ends[None, :] <= positions[:, None]).astype(jnp.int32), axis=1)
    first_pos = jnp.take(arrival_ends, sender) - jnp.take(arrivals, sender)
    slot_pick = sender * slot_count + positions - first_pos
    recv_map = (slot_pick[:, None] == slot_ids[None, :]).astype(jnp.bfloat16)
    lengths_own = enc_len.astype(jnp.float32).astype(jnp.bfloat16).reshape(block_count, 1)
    all_slots = peer_count * slot_count
    outgoing = through(send_map, enc_rows.reshape(block_count, -1), (peer_count, slot_count))
    outgoing_len = through(send_map, lengths_own, (peer_count, slot_count))
    incoming, incoming_len = (
        lax.all_to_all(outgoing, "dp", split_axis=0, concat_axis=0, tiled=True),
        lax.all_to_all(outgoing_len, "dp", split_axis=0, concat_axis=0, tiled=True),
    )
    rows_here = through(recv_map, incoming.reshape(all_slots, -1), (block_count,)).reshape(
        row_count, feature_width
    )
    lengths_here = through(recv_map, incoming_len.reshape(all_slots, 1), (block_count,))[
        :, 0
    ].astype(jnp.float32)
    shard_cols = lax.all_gather(rows_here, "mp", axis=1, tiled=True)
    key_acc = jnp.dot(shard_cols, key_full, preferred_element_type=jnp.float32)
    value_acc = jnp.dot(shard_cols, value_full, preferred_element_type=jnp.float32)
    context, key_grad, value_grad = attend(
        queries,
        key_acc.astype(jnp.bfloat16),
        value_acc.astype(jnp.bfloat16),
        ctx_grad,
        lengths_here,
    )
    col_span = key_full.shape[0] // model_groups
    pieces_out = []
    for group_idx in range(model_groups):
        key_part = key_full[group_idx * col_span : (group_idx + 1) * col_span]
        value_part = value_full[group_idx * col_span : (group_idx + 1) * col_span]
        partial_value = lax.dot_general(
            key_grad, key_part, (((1,), (1,)), ((), ())), preferred_element_type=jnp.float32
        )
        partial_value = partial_value + lax.dot_general(
            value_grad, value_part, (((1,), (1,)), ((), ())), preferred_element_type=jnp.float32
        )
        pieces_out.append(partial_value.astype(jnp.bfloat16))
    summed = lax.psum_scatter(
        jnp.concatenate(pieces_out, axis=1), "mp", scatter_dimension=1, tiled=True
    )
    outgoing_grad = through(recv_map.T, summed.reshape(block_count, -1), (peer_count, slot_count))
    returned = lax.all_to_all(outgoing_grad, "dp", split_axis=0, concat_axis=0, tiled=True)
    enc_grad = through(send_map.T, returned.reshape(all_slots, -1), (block_count,)).reshape(
        row_count, feature_width
    )
    return (context, enc_grad)


PAIR = 2 * DH
SHORT = pl.CostEstimate(flops=1, bytes_accessed=1, transcendentals=0)


def nt(a, b):
    return lax.dot_general(a, b, (((1,), (1,)), ((), ())), preferred_element_type=F32)


def tn(a, b):
    return lax.dot_general(a, b, (((0,), (0,)), ((), ())), preferred_element_type=F32)


def forward_kernel(n_dp, n_sec, n_half, blk, tab, *refs):
    blocks = n_dp * blk
    x_refs = refs[: n_half * n_dp]
    own, above, far, below, end, q_ref, g_ref, ctx_ref, dkv_ref, w_ref, acc, kv = refs[
        n_half * n_dp :
    ]
    rows = own.shape[0] // n_dp
    step = pl.program_id(0)
    z = tab[2 * blocks]
    m = tab[2 * blocks + 1]
    per_half = n_sec // n_half
    section = (m ^ (step // per_half)) * per_half + step % per_half
    hop = (section - z + n_sec) % n_sec

    @pl.when(hop == 0)
    def _():
        w_ref[...] = own[...]

    @pl.when((hop == 1) & (z != n_sec - 1))
    def _():
        w_ref[...] = above[...]

    @pl.when(hop == 2)
    def _():
        w_ref[...] = far[...]

    @pl.when((hop == n_sec - 1) & (z != 0))
    def _():
        w_ref[...] = below[...]

    @pl.when(((hop == 1) & (z == n_sec - 1)) | ((hop == n_sec - 1) & (z == 0)))
    def _():
        w_ref[...] = end[...]

    for h in range(n_half):

        @pl.when(step // per_half == h)
        def _():
            for t in range(n_dp):
                at = slice(t * rows, (t + 1) * rows)
                part = jnp.dot(
                    x_refs[h * n_dp + t][...], w_ref[...], preferred_element_type=F32
                )
                if h == 0:
                    acc[at, :] = jnp.where(step == 0, part, acc[at, :] + part)
                else:
                    acc[at, :] += part

    @pl.when(step == n_sec - 1)
    def _():
        kv[...] = acc[...].astype(BF16)
        lane = lax.broadcasted_iota(jnp.int32, (BLOCK, PAIR), 1) < DH
        key_pos = lax.broadcasted_iota(jnp.int32, (BLOCK, PAIR), 0)
        scale = DH ** (-0.5)
        zero = jnp.zeros((BLOCK, PAIR), BF16)

        def group(bs):
            source = [pl.ds(pl.multiple_of(tab[b] * BLOCK, BLOCK), BLOCK) for b in bs]
            here = [pl.ds((b % blk) * BLOCK, BLOCK) for b in bs]
            key = [kv[at, 0:PAIR] for at in source]
            value = [kv[at, PAIR : 2 * PAIR] for at in source]

            def split(ref):
                rows_of = [ref[b // blk, at, :] for b, at in zip(bs, here)]
                return [
                    jnp.concatenate([jnp.where(lane, x, zero), jnp.where(lane, zero, x)], axis=0)
                    for x in rows_of
                ]

            query = split(q_ref)
            grad = split(g_ref)
            scores = [nt(k, q) * scale for k, q in zip(key, query)]
            prob_grad = [nt(v, g) for v, g in zip(value, grad)]
            scores = [jnp.where(key_pos < tab[blocks + b], x, -1e30) for b, x in zip(bs, scores)]
            weights = [jnp.exp(x - jnp.max(x, axis=0, keepdims=True)) for x in scores]
            probs = [x / jnp.sum(x, axis=0, keepdims=True) for x in weights]
            prob_bf = [x.astype(BF16) for x in probs]
            ctx = [tn(p, v) for p, v in zip(prob_bf, value)]
            dv = [jnp.dot(p, g, preferred_element_type=F32) for p, g in zip(prob_bf, grad)]
            row_dot = [jnp.sum(p * x, axis=0, keepdims=True) for p, x in zip(probs, prob_grad)]
            score_grad = [
                (p * (x - r) * scale).astype(BF16) for p, x, r in zip(probs, prob_grad, row_dot)
            ]
            dk = [jnp.dot(x, q, preferred_element_type=F32) for x, q in zip(score_grad, query)]
            for n, b in enumerate(bs):
                ctx_ref[b // blk, here[n], :] = jnp.where(
                    lane, ctx[n][:BLOCK], ctx[n][BLOCK:]
                ).astype(BF16)
                dkv_ref[source[n], 0:PAIR] = dk[n].astype(BF16)
                dkv_ref[source[n], PAIR : 2 * PAIR] = dv[n].astype(BF16)

        for b in range(0, blocks, blk):
            group(range(b, b + blk))


def forward_chunk(table, x_pieces, pieces, q_at, g_at, blk, n_sec, n_dp):
    n_half = len(x_pieces) // n_dp
    cols = pieces[0].shape[1]
    rows = pieces[0].shape[0] // n_dp
    per_half = n_sec // n_half
    span = x_pieces[0][0].shape[1] // per_half

    def x_spec(h, row):
        return pl.BlockSpec(
            (rows, span), lambda a, t: (row, jnp.clip(a - h * per_half, 0, per_half - 1))
        )

    whole = pl.BlockSpec((span, cols), lambda a, t: (0, 0))

    def head(at):
        return pl.BlockSpec((n_dp, rows, PAIR), lambda a, t: (0, 0, at))

    return pl.pallas_call(
        functools.partial(forward_kernel, n_dp, n_sec, n_half, blk),
        grid_spec=pltpu.PrefetchScalarGridSpec(
            num_scalar_prefetch=1,
            grid=(n_sec,),
            in_specs=[x_spec(i // n_dp, row) for i, (_, row) in enumerate(x_pieces)]
            + [whole] * 5
            + [head(q_at[1]), head(g_at[1])],
            out_specs=[
                head(0),
                pl.BlockSpec((n_dp * rows, cols), lambda a, t: (0, 0)),
                pl.BlockSpec((span, cols), lambda a, t: (a, 0)),
            ],
            scratch_shapes=[
                pltpu.VMEM((n_dp * rows, cols), F32),
                pltpu.VMEM((n_dp * rows, cols), BF16),
            ],
        ),
        out_shape=[
            jax.ShapeDtypeStruct((n_dp, rows, PAIR), BF16),
            jax.ShapeDtypeStruct((n_dp * rows, cols), BF16),
            jax.ShapeDtypeStruct((n_sec * span, cols), BF16),
        ],
        compiler_params=pltpu.CompilerParams(vmem_limit_bytes=60 << 20),
        cost_estimate=SHORT,
        name="fwd",
    )(table, *[x for x, _ in x_pieces], *pieces, q_at[0], g_at[0])


def backward_kernel(chunks, add, *refs):
    out_ref = refs[-1]
    total = nt(refs[0][...], refs[chunks][...])
    for c in range(1, chunks):
        total += nt(refs[c][...], refs[chunks + c][...])
    if add:
        total += refs[2 * chunks][...].astype(F32)
    out_ref[...] = total.astype(out_ref.dtype)


def backward(dkvs, ws, rows, span, row_at, row_n, col_at, col_n, received, out_dtype):
    chunks = len(dkvs)
    cols = dkvs[0].shape[1]
    specs = [pl.BlockSpec((rows, cols), lambda h, r: (row_at + 2 * r, 0))] * chunks
    specs += [pl.BlockSpec((span, cols), lambda h, r: (col_at + 2 * h, 0))] * chunks
    block = pl.BlockSpec((rows, span), lambda h, r: (r, h))
    extra = () if received is None else (received,)
    return pl.pallas_call(
        functools.partial(backward_kernel, chunks, received is not None),
        grid=(col_n, row_n),
        in_specs=specs + [block] * len(extra),
        out_specs=block,
        out_shape=jax.ShapeDtypeStruct((row_n * rows, col_n * span), out_dtype),
        compiler_params=pltpu.CompilerParams(vmem_limit_bytes=48 << 20),
        cost_estimate=SHORT,
        name="bwd",
    )(*dkvs, *ws, *extra)


def finish_kernel(p_ref, got_y, last_x, q_ref, got_x, last_y, out):
    span = out.shape[1] // 2
    out[:, :span] = (
        p_ref[...] + got_y[...].astype(F32) + last_x[...].astype(F32)
    ).astype(BF16)
    out[:, span:] = (
        q_ref[...] + got_x[...].astype(F32) + last_y[...].astype(F32)
    ).astype(BF16)


def finish(*operands):
    rows, span = operands[2].shape
    block = pl.BlockSpec((rows, span), lambda i: (0, 0))
    return pl.pallas_call(
        finish_kernel,
        grid=(1,),
        in_specs=[block] * 6,
        out_specs=pl.BlockSpec((rows, 2 * span), lambda i: (0, 0)),
        out_shape=jax.ShapeDtypeStruct((rows, 2 * span), BF16),
        name="finish",
    )(*operands)


def context_kernel(*refs):
    out = refs[-1]
    at = 0
    for ref in refs[:-1]:
        out[:, at : at + ref.shape[2]] = ref[0]
        at += ref.shape[2]


def gather_context(*parts):
    n_dp, rows = parts[0].shape[:2]
    cols = sum(part.shape[2] for part in parts)
    return pl.pallas_call(
        context_kernel,
        grid=(n_dp,),
        in_specs=[pl.BlockSpec((1, rows, part.shape[2]), lambda j: (j, 0, 0)) for part in parts],
        out_specs=pl.BlockSpec((rows, cols), lambda j: (0, j)),
        out_shape=jax.ShapeDtypeStruct((rows, n_dp * cols), BF16),
        name="gather_context",
    )(*parts)


def shards_section(enc_rows, enc_len, dest_dp, peer_counts, queries, ctx_grad, w_key, w_value):
    n_sec, n_dp, n_mp = (lax.axis_size(a) for a in ("section", "dp", "mp"))
    z, d, m = (lax.axis_index(a).astype(jnp.int32) for a in ("section", "dp", "mp"))
    blk = dest_dp.shape[0]
    blocks = blk * n_dp
    rows, half = enc_rows.shape
    head_cols = w_key.shape[1] // n_dp

    core = [(i, i ^ 1) for i in range(n_dp)]
    ypairs = [(i, i ^ 2) for i in range(n_dp)]
    xpairs = [(0, 1), (1, 0)]
    up = [(i, i + 1) for i in range(n_sec - 1)]
    down = [(i + 1, i) for i in range(n_sec - 1)]
    over_two = [(i, i ^ 2) for i in range(n_sec)]
    ends = [(1, 0), (2, 3)]
    outer = [(0, n_sec - 1), (n_sec - 1, 0)]

    def step(waited, released=()):
        return lax.optimization_barrier((tuple(waited), tuple(released)))

    def swap(x):
        return lax.ppermute(x, "dp", core)

    def exchange(x):
        return lax.all_to_all(x, "dp", split_axis=0, concat_axis=0, tiled=True)

    def by_owner(x):
        return x.reshape(rows, n_dp, head_cols).transpose(1, 0, 2)

    def weight_parts(c, *ws):
        return jnp.concatenate([by_owner(w)[:, :, c * PAIR : (c + 1) * PAIR] for w in ws], axis=2)

    def along(piece):
        return (
            lax.ppermute(piece, "section", up),
            lax.ppermute(piece, "section", down),
            lax.ppermute(piece, "section", over_two),
        )

    own0 = exchange(weight_parts(0, w_key, w_value)).reshape(n_dp * rows, 2 * PAIR)
    e_x = lax.ppermute(enc_rows, "mp", xpairs)
    e_c = swap(enc_rows)

    (own0, e_c), (e, w_k, w_v, q_in, g_in) = step(
        (own0, e_c), (enc_rows, w_key, w_value, queries, ctx_grad)
    )
    z0 = along(own0)
    e_y = lax.ppermute(e, "dp", ypairs)
    own1 = exchange(weight_parts(1, w_k, w_v)).reshape(n_dp * rows, 2 * PAIR)
    parts = jnp.concatenate(
        [by_owner(q_in), by_owner(g_in), weight_parts(2, w_k, w_v), weight_parts(3, w_k, w_v)],
        axis=2,
    )
    small = jnp.concatenate([enc_len, dest_dp, peer_counts[0]]).astype(BF16)
    small = jnp.pad(small[None, :], ((0, 15), (0, parts.shape[2] - small.shape[0])))
    small = jnp.broadcast_to(small[None], (n_dp,) + small.shape)
    parts = jnp.concatenate([parts, small], axis=1)

    (z0, own1, e_y, e_x, parts), _ = step((z0, own1, e_y, e_x, parts))
    end0 = lax.ppermute(z0[2], "section", ends)
    z1 = along(own1)
    e_yx = lax.ppermute(e_y, "mp", xpairs)
    got = exchange(parts)
    e_xy = jnp.concatenate([e_x, e_y], axis=0)

    (end0, z1, e_yx, e_xy, got), _ = step((end0, z1, e_yx, e_xy, got))
    own2, own3 = (
        got[:, :rows, 2 * head_cols + 2 * PAIR * i : 2 * head_cols + 2 * PAIR * (i + 1)].reshape(
            n_dp * rows, 2 * PAIR
        )
        for i in range(2)
    )
    end1 = lax.ppermute(z1[2], "section", ends)
    z2 = along(own2)
    e_xyc, e_yxc = swap(e_xy), swap(e_yx)

    packs = got[:, rows, : 2 * blk + n_dp].astype(jnp.int32)
    lens = packs[:, :blk].reshape(-1)
    dest = packs[:, blk : 2 * blk]
    counts = packs[:, 2 * blk :]
    peer = jnp.arange(n_dp, dtype=jnp.int32)
    pos = jnp.arange(blk, dtype=jnp.int32)
    before = jnp.sum(
        jnp.where(peer[None, None, :] < peer[None, :, None], counts[:, None, :], 0), axis=2
    )
    upto = before + counts
    sender = jnp.sum((upto[:, None, :] <= pos[None, :, None]).astype(jnp.int32), axis=2)
    is_sender = sender[:, :, None] == peer[None, None, :]
    rank = pos[None, :] - jnp.sum(jnp.where(is_sender, before[:, None, :], 0), axis=2)
    same = dest[:, :, None] == dest[:, None, :]
    slot_rank = jnp.sum((same & (pos[None, None, :] < pos[None, :, None])).astype(jnp.int32), axis=2)
    hit = (
        is_sender[:, :, :, None]
        & (dest[None, None] == peer[:, None, None, None])
        & (slot_rank[None, None] == rank[:, :, None, None])
    ).reshape(blocks, blocks)
    place = ((peer ^ d)[:, None] * blk + pos[None, :]).reshape(-1)
    src = jnp.sum(jnp.where(hit, place[None, :], 0), axis=1)
    src_len = jnp.sum(jnp.where(hit, lens[None, :], 0), axis=1)
    table = jnp.concatenate([src, src_len, jnp.stack([z, m])])

    x_pieces = [(e, 0), (e_c, 0), (e_y, 0), (e_xyc, 1)]
    x_pieces += [(e_x, 0), (e_xyc, 0), (e_yx, 0), (e_yxc, 0)]
    q_blocks = head_cols // PAIR

    def forward(c, own, zs, end):
        up_, down_, far = zs
        return forward_chunk(
            table,
            x_pieces,
            (own, down_, far, up_, end),
            (got, c),
            (got, q_blocks + c),
            blk,
            n_sec,
            n_dp,
        )

    f0 = forward(0, own0, z0, end0)

    (end1, z2, own3, f0), _ = step((end1, z2, own3, f0))
    end2 = lax.ppermute(z2[2], "section", ends)
    z3 = along(own3)
    end3 = lax.ppermute(own3, "section", outer)
    f1 = forward(1, own1, z1, end1)
    context_a = exchange(jnp.concatenate([f0[0], f1[0]], axis=2))
    f2 = forward(2, own2, z2, end2)

    (z3, end3, f1, f2, context_a), _ = step((z3, end3, f1, f2, context_a))
    f3 = forward(3, own3, z3, end3)
    context_b = exchange(jnp.concatenate([f2[0], f3[0]], axis=2))

    dkvs = tuple(f[1] for f in (f0, f1, f2, f3))
    ws = tuple(f[2] for f in (f0, f1, f2, f3))
    span = half // (n_sec // n_mp)
    give_y = swap(backward(dkvs, ws, rows, span, 3, 1, 0, 2, None, BF16))
    give_x = swap(backward(dkvs, ws, rows, span, 1, 2, 3, 1, None, BF16))
    send_y = backward(dkvs, ws, rows, span, 2, 1, 0, 2, give_y, BF16)
    send_x = backward(dkvs, ws, rows, span, 0, 2, 3, 1, give_x, BF16)
    (send_y, send_x, context_b), dkvs = step((send_y, send_x, context_b), dkvs)
    got_y = lax.ppermute(send_y, "dp", ypairs)
    got_x = lax.ppermute(send_x, "mp", xpairs)
    give_p = swap(backward(dkvs, ws, rows, span, 1, 1, 0, 2, None, BF16))
    give_q = swap(backward(dkvs, ws, rows, span, 1, 2, 1, 1, None, BF16))
    p_own = backward(dkvs, ws, rows, span, 0, 1, 0, 2, give_p, F32)
    q_own = backward(dkvs, ws, rows, span, 0, 2, 1, 1, give_q, F32)
    context = gather_context(context_a, context_b)
    got_y, got_x, p_own, q_own, context = lax.optimization_barrier(
        (got_y, got_x, p_own, q_own, context)
    )
    to_x = (p_own[:, span:] + got_y[:, span:].astype(F32)).astype(BF16)
    to_y = (q_own[rows:] + got_x[rows:].astype(F32)).astype(BF16)
    last_x = lax.ppermute(to_x, "mp", xpairs)
    last_y = lax.ppermute(to_y, "dp", ypairs)
    enc_grad = finish(p_own, got_y, last_x, q_own, got_x, last_y)
    return (context, enc_grad)


def solution(mesh):
    placed = (
        P(("section", "dp"), "mp"),
        P(("section", "dp")),
        P(("section", "dp")),
        P(("section", "dp"), None),
        P(("section", "dp"), "mp"),
        P(("section", "dp"), "mp"),
        P(("section", "dp"), "mp"),
        P(("section", "dp"), "mp"),
    )
    sizes = tuple(mesh.shape[a] for a in ("section", "dp", "mp"))
    body = shards_section if sizes == (4, 4, 2) else shards_general
    return jax.shard_map(
        body,
        mesh=mesh,
        in_specs=placed,
        out_specs=(P(("section", "dp"), "mp"), P(("section", "dp"), "mp")),
        check_vma=False,
    )
```

```python
import functools

import jax
import jax.numpy as jnp
from jax import lax
from jax.experimental import pallas as pl
from jax.experimental.pallas import tpu as pltpu
from jax.sharding import PartitionSpec as P

DH = 64
BLOCK = 64
F32 = jnp.float32
BF16 = jnp.bfloat16


def attend(query_rows, key_rows, value_rows, grad_rows, key_lengths):
    block_count = key_lengths.shape[0]
    head_count = query_rows.shape[1] // DH
    shape_four = (block_count, BLOCK, head_count, DH)
    query_heads = query_rows.reshape(shape_four)
    key_heads = key_rows.reshape(shape_four)
    value_heads = value_rows.reshape(shape_four)
    grad_heads = grad_rows.reshape(shape_four)
    score_scale = DH ** (-0.5)
    scores = (
        jnp.einsum("bihd,bjhd->bhij", query_heads, key_heads, preferred_element_type=jnp.float32)
        * score_scale
    )
    visible = (
        jnp.arange(BLOCK, dtype=jnp.float32)[None, None, None, :] < key_lengths[:, None, None, None]
    )
    scores = jnp.where(visible, scores, -1e30)
    row_max = jnp.max(scores, axis=-1, keepdims=True)
    weights_exp = jnp.exp(scores - row_max)
    probabilities = weights_exp / jnp.sum(weights_exp, axis=-1, keepdims=True)
    prob_bf = probabilities.astype(jnp.bfloat16)
    context = jnp.einsum(
        "bhij,bjhd->bihd", prob_bf, value_heads, preferred_element_type=jnp.float32
    ).astype(jnp.bfloat16)
    prob_grad = jnp.einsum(
        "bihd,bjhd->bhij", grad_heads, value_heads, preferred_element_type=jnp.float32
    )
    row_dot = jnp.sum(probabilities * prob_grad, axis=-1, keepdims=True)
    score_grad = (probabilities * (prob_grad - row_dot) * score_scale).astype(jnp.bfloat16)
    key_grad = jnp.einsum(
        "bhij,bihd->bjhd", score_grad, query_heads, preferred_element_type=jnp.float32
    ).astype(jnp.bfloat16)
    value_grad = jnp.einsum(
        "bhij,bihd->bjhd", prob_bf, grad_heads, preferred_element_type=jnp.float32
    ).astype(jnp.bfloat16)
    flat_shape = (block_count * BLOCK, head_count * DH)
    return (
        context.reshape(flat_shape),
        key_grad.reshape(flat_shape),
        value_grad.reshape(flat_shape),
    )


def through(table, data, lead_shape):
    moved = jnp.dot(table, data, preferred_element_type=jnp.float32).astype(jnp.bfloat16)
    return moved.reshape(lead_shape + data.shape[1:])


def shards_general(enc_rows, enc_len, dest_dp, peer_counts, queries, ctx_grad, w_key, w_value):
    peer_count = lax.axis_size("dp")
    model_groups = lax.axis_size("mp")
    block_count = dest_dp.shape[0]
    slot_count = max(2, -(-block_count // peer_count))
    row_count, feature_width = enc_rows.shape
    key_full, value_full = (
        lax.all_gather(w_key, ("section", "dp"), axis=0, tiled=True),
        lax.all_gather(w_value, ("section", "dp"), axis=0, tiled=True),
    )
    positions = jnp.arange(block_count, dtype=jnp.int32)
    same_dest = dest_dp[:, None] == dest_dp[None, :]
    slot_rank = jnp.sum(
        (same_dest & (positions[None, :] < positions[:, None])).astype(jnp.int32), axis=1
    )
    target_slot = dest_dp * slot_count + slot_rank
    slot_ids = jnp.arange(peer_count * slot_count, dtype=jnp.int32)
    send_map = (slot_ids[:, None] == target_slot[None, :]).astype(jnp.bfloat16)
    arrivals = peer_counts[0]
    arrival_ends = jnp.cumsum(arrivals)
    sender = jnp.sum((arrival_ends[None, :] <= positions[:, None]).astype(jnp.int32), axis=1)
    first_pos = jnp.take(arrival_ends, sender) - jnp.take(arrivals, sender)
    slot_pick = sender * slot_count + positions - first_pos
    recv_map = (slot_pick[:, None] == slot_ids[None, :]).astype(jnp.bfloat16)
    lengths_own = enc_len.astype(jnp.float32).astype(jnp.bfloat16).reshape(block_count, 1)
    all_slots = peer_count * slot_count
    outgoing = through(send_map, enc_rows.reshape(block_count, -1), (peer_count, slot_count))
    outgoing_len = through(send_map, lengths_own, (peer_count, slot_count))
    incoming, incoming_len = (
        lax.all_to_all(outgoing, "dp", split_axis=0, concat_axis=0, tiled=True),
        lax.all_to_all(outgoing_len, "dp", split_axis=0, concat_axis=0, tiled=True),
    )
    rows_here = through(recv_map, incoming.reshape(all_slots, -1), (block_count,)).reshape(
        row_count, feature_width
    )
    lengths_here = through(recv_map, incoming_len.reshape(all_slots, 1), (block_count,))[
        :, 0
    ].astype(jnp.float32)
    shard_cols = lax.all_gather(rows_here, "mp", axis=1, tiled=True)
    key_acc = jnp.dot(shard_cols, key_full, preferred_element_type=jnp.float32)
    value_acc = jnp.dot(shard_cols, value_full, preferred_element_type=jnp.float32)
    context, key_grad, value_grad = attend(
        queries,
        key_acc.astype(jnp.bfloat16),
        value_acc.astype(jnp.bfloat16),
        ctx_grad,
        lengths_here,
    )
    col_span = key_full.shape[0] // model_groups
    pieces_out = []
    for group_idx in range(model_groups):
        key_part = key_full[group_idx * col_span : (group_idx + 1) * col_span]
        value_part = value_full[group_idx * col_span : (group_idx + 1) * col_span]
        partial_value = lax.dot_general(
            key_grad, key_part, (((1,), (1,)), ((), ())), preferred_element_type=jnp.float32
        )
        partial_value = partial_value + lax.dot_general(
            value_grad, value_part, (((1,), (1,)), ((), ())), preferred_element_type=jnp.float32
        )
        pieces_out.append(partial_value.astype(jnp.bfloat16))
    summed = lax.psum_scatter(
        jnp.concatenate(pieces_out, axis=1), "mp", scatter_dimension=1, tiled=True
    )
    outgoing_grad = through(recv_map.T, summed.reshape(block_count, -1), (peer_count, slot_count))
    returned = lax.all_to_all(outgoing_grad, "dp", split_axis=0, concat_axis=0, tiled=True)
    enc_grad = through(send_map.T, returned.reshape(all_slots, -1), (block_count,)).reshape(
        row_count, feature_width
    )
    return (context, enc_grad)


PAIR = 2 * DH
SLOTS = (0, 2, 1, 3)
SHORT = pl.CostEstimate(flops=1, bytes_accessed=1, transcendentals=0)


def nt(a, b):
    return lax.dot_general(a, b, (((1,), (1,)), ((), ())), preferred_element_type=F32)


def tn(a, b):
    return lax.dot_general(a, b, (((0,), (0,)), ((), ())), preferred_element_type=F32)


def forward_kernel(n_dp, n_sec, n_half, blk, tab, *refs):
    blocks = n_dp * blk
    x_refs = refs[: n_half * n_dp]
    own, above, far, below, end = refs[n_half * n_dp : n_half * n_dp + 5]
    q_ref, g_ref = refs[n_half * n_dp + 5 : n_half * n_dp + 7]
    ctx_ref, dkv_ref, w_ref, acc, kv = refs[-5:]
    rows = acc.shape[0] // n_dp
    step = pl.program_id(0)
    per_half = n_sec // n_half
    z = tab[2 * blocks]
    m = tab[2 * blocks + 1]
    section = (m ^ (step // per_half)) * per_half + step % per_half
    hop = (section - z + n_sec) % n_sec

    def take(ref):
        w_ref[...] = ref[...].reshape(w_ref.shape)

    @pl.when(hop == 0)
    def _():
        take(own)

    @pl.when((hop == 1) & (z != n_sec - 1))
    def _():
        take(above)

    @pl.when(hop == 2)
    def _():
        take(far)

    @pl.when((hop == n_sec - 1) & (z != 0))
    def _():
        take(below)

    @pl.when(((hop == 1) & (z == n_sec - 1)) | ((hop == n_sec - 1) & (z == 0)))
    def _():
        take(end)

    for h in range(n_half):

        @pl.when(step // per_half == h)
        def _():
            for t in range(n_dp):
                at = slice(t * rows, (t + 1) * rows)
                part = jnp.dot(
                    x_refs[h * n_dp + t][0], w_ref[...], preferred_element_type=F32
                )
                if h == 0:
                    acc[at, :] = jnp.where(step == 0, part, acc[at, :] + part)
                else:
                    acc[at, :] += part

    @pl.when(step == n_sec - 1)
    def _():
        kv[...] = acc[...].astype(BF16)
        lane = lax.broadcasted_iota(jnp.int32, (BLOCK, PAIR), 1) < DH
        key_pos = lax.broadcasted_iota(jnp.int32, (BLOCK, PAIR), 0)
        scale = DH ** (-0.5)
        zero = jnp.zeros((BLOCK, PAIR), BF16)

        def group(bs):
            source = [pl.ds(pl.multiple_of(tab[b] * BLOCK, BLOCK), BLOCK) for b in bs]
            here = [pl.ds((b % blk) * BLOCK, BLOCK) for b in bs]
            key = [kv[at, 0:PAIR] for at in source]
            value = [kv[at, PAIR : 2 * PAIR] for at in source]

            def split(ref):
                rows_of = [ref[b // blk, at, :] for b, at in zip(bs, here)]
                return [
                    jnp.concatenate([jnp.where(lane, x, zero), jnp.where(lane, zero, x)], axis=0)
                    for x in rows_of
                ]

            query = split(q_ref)
            grad = split(g_ref)
            scores = [nt(k, q) * scale for k, q in zip(key, query)]
            prob_grad = [nt(v, g) for v, g in zip(value, grad)]
            scores = [jnp.where(key_pos < tab[blocks + b], x, -1e30) for b, x in zip(bs, scores)]
            weights = [jnp.exp(x - jnp.max(x, axis=0, keepdims=True)) for x in scores]
            probs = [x / jnp.sum(x, axis=0, keepdims=True) for x in weights]
            prob_bf = [x.astype(BF16) for x in probs]
            ctx = [tn(p, v) for p, v in zip(prob_bf, value)]
            dv = [jnp.dot(p, g, preferred_element_type=F32) for p, g in zip(prob_bf, grad)]
            row_dot = [jnp.sum(p * x, axis=0, keepdims=True) for p, x in zip(probs, prob_grad)]
            score_grad = [
                (p * (x - r) * scale).astype(BF16) for p, x, r in zip(probs, prob_grad, row_dot)
            ]
            dk = [jnp.dot(x, q, preferred_element_type=F32) for x, q in zip(score_grad, query)]
            for n, b in enumerate(bs):
                ctx_ref[b // blk, here[n], :] = jnp.where(
                    lane, ctx[n][:BLOCK], ctx[n][BLOCK:]
                ).astype(BF16)
                dkv_ref[source[n], 0:PAIR] = dk[n].astype(BF16)
                dkv_ref[source[n], PAIR : 2 * PAIR] = dv[n].astype(BF16)

        for b in range(0, blocks, blk):
            group(range(b, b + blk))


def forward_chunk(table, x, pieces, got, chunk, chunks, blk, n_sec, n_dp, before):
    n_half = x.shape[0] // n_dp
    cols = 2 * PAIR
    per_half = n_sec // n_half
    span = x.shape[2] // per_half
    rows = span // n_dp
    scalars = 2 * n_dp * blk

    def x_spec(h, slot):
        def at(a, t):
            sender = (t[scalars + 2] ^ slot) * n_half + (t[scalars + 1] ^ h)
            return (sender, 0, jnp.clip(a - h * per_half, 0, per_half - 1))

        return pl.BlockSpec((1, rows, span), at)

    def fixed(shape, at):
        return pl.BlockSpec(shape, lambda a, t: at)

    def head(at):
        return pl.BlockSpec((n_dp, rows, PAIR), lambda a, t: (0, 0, at))

    operands = [table] + [x] * (n_half * n_dp) + [p[0] for p in pieces] + [got, got]
    in_specs = [x_spec(h, slot) for h in range(n_half) for slot in SLOTS]
    in_specs += [fixed(shape, at) for _, shape, at in pieces]
    in_specs += [head(chunk), head(chunks + chunk)]
    aliases = {}
    if before is not None:
        aliases = {len(operands): 1, len(operands) + 1: 2}
        operands += before
        in_specs += [pl.BlockSpec(memory_space=pl.ANY)] * 2
    return pl.pallas_call(
        functools.partial(forward_kernel, n_dp, n_sec, n_half, blk),
        grid_spec=pltpu.PrefetchScalarGridSpec(
            num_scalar_prefetch=1,
            grid=(n_sec,),
            in_specs=in_specs,
            out_specs=[
                head(0),
                pl.BlockSpec((n_dp * rows, cols), lambda a, t: (0, chunk)),
                pl.BlockSpec((span, cols), lambda a, t: (a, chunk)),
            ],
            scratch_shapes=[
                pltpu.VMEM((n_dp * rows, cols), F32),
                pltpu.VMEM((n_dp * rows, cols), BF16),
            ],
        ),
        out_shape=[
            jax.ShapeDtypeStruct((n_dp, rows, PAIR), BF16),
            jax.ShapeDtypeStruct((n_dp * rows, chunks * cols), BF16),
            jax.ShapeDtypeStruct((n_sec * span, chunks * cols), BF16),
        ],
        input_output_aliases=aliases,
        compiler_params=pltpu.CompilerParams(vmem_limit_bytes=60 << 20),
        cost_estimate=SHORT,
        name="fwd",
    )(*operands)


def backward_kernel(*refs):
    total = nt(refs[0][...], refs[1][...])
    for ref in refs[2:-1]:
        total += ref[...].astype(F32)
    refs[-1][...] = total.astype(refs[-1].dtype)


def backward(dkv, w, received, rows, cols, out_dtype):
    row_n, row_at = rows
    span, blocks = cols
    depth = dkv.shape[1]
    tile = 512
    per_block = span // tile

    def col(i):
        at = blocks[0]
        for k in range(1, len(blocks)):
            at = jnp.where(i >= k * per_block, blocks[k], at)
        return at * per_block + i % per_block

    specs = [
        pl.BlockSpec((row_n, depth), lambda i: (row_at, 0)),
        pl.BlockSpec((tile, depth), lambda i: (col(i), 0)),
    ]
    extra = ()
    if received is not None:
        array, add_row, add_col = received
        specs.append(
            pl.BlockSpec((row_n, tile), lambda i: (add_row, add_col * per_block + i))
        )
        extra = (array,)
    return pl.pallas_call(
        backward_kernel,
        grid=(len(blocks) * per_block,),
        in_specs=specs,
        out_specs=pl.BlockSpec((row_n, tile), lambda i: (0, i)),
        out_shape=jax.ShapeDtypeStruct((row_n, len(blocks) * span), out_dtype),
        compiler_params=pltpu.CompilerParams(vmem_limit_bytes=60 << 20),
        cost_estimate=SHORT,
        name="bwd",
    )(dkv, w, *extra)


def finish_kernel(p_ref, got_y, last_x, q_ref, got_x, last_y, out):
    span = out.shape[1] // 2
    out[:, :span] = (
        p_ref[...] + got_y[...].astype(F32) + last_x[...].astype(F32)
    ).astype(BF16)
    out[:, span:] = (
        q_ref[...] + got_x[...].astype(F32) + last_y[...].astype(F32)
    ).astype(BF16)


def finish(*operands):
    rows, span = operands[2].shape
    tiles = 2
    block = pl.BlockSpec((rows // tiles, span), lambda i: (i, 0))
    return pl.pallas_call(
        finish_kernel,
        grid=(tiles,),
        in_specs=[block] * 6,
        out_specs=pl.BlockSpec((rows // tiles, 2 * span), lambda i: (i, 0)),
        out_shape=jax.ShapeDtypeStruct((rows, 2 * span), BF16),
        cost_estimate=SHORT,
        name="finish",
    )(*operands)


def weight_kernel(k_ref, v_ref, out):
    out[0, :, :PAIR] = k_ref[...]
    out[0, :, PAIR:] = v_ref[...]


def pack_weights(w_key, w_value, chunk, n_dp):
    rows, width = w_key.shape
    per_owner = width // n_dp // PAIR
    block = pl.BlockSpec((rows, PAIR), lambda j: (0, j * per_owner + chunk))
    return pl.pallas_call(
        weight_kernel,
        grid=(n_dp,),
        in_specs=[block] * 2,
        out_specs=pl.BlockSpec((1, rows, 2 * PAIR), lambda j: (j, 0, 0)),
        out_shape=jax.ShapeDtypeStruct((n_dp, rows, 2 * PAIR), BF16),
        cost_estimate=SHORT,
        name="pack_weights",
    )(w_key, w_value)


def pack_kernel(q_ref, g_ref, k_ref, v_ref, small_ref, out):
    rows, cols = q_ref.shape
    parts = [q_ref[...], g_ref[...]]
    for c in range(0, k_ref.shape[1], PAIR):
        parts += [k_ref[:, c : c + PAIR], v_ref[:, c : c + PAIR]]
    at = 0
    for part in parts:
        out[0, :rows, at : at + part.shape[1]] = part
        at += part.shape[1]
    out[0, rows:, :] = jnp.zeros((out.shape[1] - rows, out.shape[2]), BF16)
    out[0, rows:, :PAIR] = small_ref[...]


def pack(queries, grads, w_key, w_value, small, n_dp):
    rows, width = queries.shape
    cols = width // n_dp
    block = pl.BlockSpec((rows, cols), lambda j: (0, j))
    tail = pl.BlockSpec((rows, cols // 2), lambda j: (0, 2 * j + 1))
    extra = small.shape[0]
    return pl.pallas_call(
        pack_kernel,
        grid=(n_dp,),
        in_specs=[block, block, tail, tail, pl.BlockSpec(small.shape, lambda j: (0, 0))],
        out_specs=pl.BlockSpec((1, rows + extra, 3 * cols), lambda j: (j, 0, 0)),
        out_shape=jax.ShapeDtypeStruct((n_dp, rows + extra, 3 * cols), BF16),
        cost_estimate=SHORT,
        name="pack",
    )(queries, grads, w_key, w_value, small)


def context_kernel(n_dp, tab, early, *refs):
    out = refs[-1]
    cols = early.shape[2]
    out[:, :cols] = early[0]
    for t in range(n_dp):

        @pl.when(pl.program_id(0) == t)
        def _():
            out[:, cols:] = refs[t][...]


def gather_context(d, early, late):
    n_dp, rows, cols = early.shape
    last = late[0].shape[1]
    return pl.pallas_call(
        functools.partial(context_kernel, n_dp),
        grid_spec=pltpu.PrefetchScalarGridSpec(
            num_scalar_prefetch=1,
            grid=(n_dp,),
            in_specs=[pl.BlockSpec((1, rows, cols), lambda t, tab: (tab[0] ^ t, 0, 0))]
            + [pl.BlockSpec((rows, last), lambda t, tab: (0, 0))] * n_dp,
            out_specs=pl.BlockSpec((rows, cols + last), lambda t, tab: (0, tab[0] ^ t)),
        ),
        out_shape=jax.ShapeDtypeStruct((rows, n_dp * (cols + last)), BF16),
        cost_estimate=SHORT,
        name="gather_context",
    )(d.reshape(1), early, *late)


def shards_section(enc_rows, enc_len, dest_dp, peer_counts, queries, ctx_grad, w_key, w_value):
    n_sec, n_dp, n_mp = (lax.axis_size(a) for a in ("section", "dp", "mp"))
    z, d, m = (lax.axis_index(a).astype(jnp.int32) for a in ("section", "dp", "mp"))
    blk = dest_dp.shape[0]
    blocks = blk * n_dp
    rows, half = enc_rows.shape
    head_cols = w_key.shape[1] // n_dp

    core = [(i, i ^ 1) for i in range(n_dp)]
    ypairs = [(i, i ^ 2) for i in range(n_dp)]
    xpairs = [(0, 1), (1, 0)]
    up = [(i, i + 1) for i in range(n_sec - 1)]
    down = [(i + 1, i) for i in range(n_sec - 1)]
    over_two = [(i, i ^ 2) for i in range(n_sec)]
    ends = [(1, 0), (2, 3)]
    outer = [(0, n_sec - 1), (n_sec - 1, 0)]

    def step(*waited, released=()):
        done = ()
        for group in waited:
            done = done + (tuple(group),)
            if group is not waited[-1]:
                done = lax.optimization_barrier(done)
        done, released = lax.optimization_barrier((done, tuple(released)))
        return (*done, released)

    def swap(x):
        return lax.ppermute(x, "dp", core)

    def exchange(x):
        return lax.all_to_all(x, "dp", split_axis=0, concat_axis=0, tiled=True)

    def sides(piece):
        return lax.ppermute(piece, "section", up), lax.ppermute(piece, "section", down)

    def beyond(piece):
        return lax.ppermute(piece, "section", over_two)

    def turn(far):
        return lax.ppermute(far, "section", ends)

    def flat(x):
        return x.reshape(n_dp * rows, 2 * PAIR)

    own0 = flat(exchange(pack_weights(w_key, w_value, 0, n_dp)))
    x = lax.all_gather(enc_rows, ("dp", "mp"), axis=0, tiled=False)
    small = jnp.concatenate([enc_len, dest_dp, peer_counts[0]]).astype(BF16)
    small = jnp.pad(small[None, :], ((0, 15), (0, PAIR - small.shape[0])))

    (own0,), (w_k, w_v) = step((own0,), released=(w_key, w_value))
    near0, far0 = sides(own0), beyond(own0)
    own1 = flat(exchange(pack_weights(w_k, w_v, 1, n_dp)))
    parts = pack(queries, ctx_grad, w_k, w_v, small, n_dp)

    (far0,), near0, (own1, parts), _ = step((far0,), near0, (own1, parts))
    near1, far1, end0 = sides(own1), beyond(own1), turn(far0)
    got = exchange(parts)

    (end0,), (far1,), near1, (x, got), _ = step((end0,), (far1,), near1, (x, got))
    own2, own3 = (
        flat(got[:, :rows, 2 * head_cols + 2 * PAIR * i : 2 * head_cols + 2 * PAIR * (i + 1)])
        for i in range(2)
    )
    near2, far2, end1 = sides(own2), beyond(own2), turn(far1)

    packs = got[:, rows, : 2 * blk + n_dp].astype(jnp.int32)
    lens = packs[:, :blk].reshape(-1)
    dest = packs[:, blk : 2 * blk]
    counts = packs[:, 2 * blk :]
    peer = jnp.arange(n_dp, dtype=jnp.int32)
    pos = jnp.arange(blk, dtype=jnp.int32)
    before = jnp.sum(
        jnp.where(peer[None, None, :] < peer[None, :, None], counts[:, None, :], 0), axis=2
    )
    upto = before + counts
    sender = jnp.sum((upto[:, None, :] <= pos[None, :, None]).astype(jnp.int32), axis=2)
    is_sender = sender[:, :, None] == peer[None, None, :]
    rank = pos[None, :] - jnp.sum(jnp.where(is_sender, before[:, None, :], 0), axis=2)
    same = dest[:, :, None] == dest[:, None, :]
    slot_rank = jnp.sum((same & (pos[None, None, :] < pos[None, :, None])).astype(jnp.int32), axis=2)
    hit = (
        is_sender[:, :, :, None]
        & (dest[None, None] == peer[:, None, None, None])
        & (slot_rank[None, None] == rank[:, :, None, None])
    ).reshape(blocks, blocks)
    gap = peer ^ d
    gap = jnp.where(gap == 1, 2, jnp.where(gap == 2, 1, gap))
    place = (gap[:, None] * blk + pos[None, :]).reshape(-1)
    src = jnp.sum(jnp.where(hit, place[None, :], 0), axis=1)
    src_len = jnp.sum(jnp.where(hit, lens[None, :], 0), axis=1)
    table = jnp.concatenate([src, src_len, jnp.stack([z, m, d])])

    chunks = head_cols // PAIR

    def forward(c, own, near, far, end, before):
        pieces = [(x, x.shape, (0, 0)) for x in (own, near[1], far, near[0], end)]
        return forward_chunk(
            table, x, pieces, got, c, chunks, blk, n_sec, n_dp, before
        )

    f0 = forward(0, own0, near0, far0, end0, None)

    (end1,), (far2,), near2, (own3, f0), _ = step((end1,), (far2,), near2, (own3, f0))
    near3, far3, end2 = sides(own3), beyond(own3), turn(far2)
    end3 = lax.ppermute(own3, "section", outer)
    f1 = forward(1, own1, near1, far1, end1, f0[1:])
    context_a = exchange(jnp.concatenate([f0[0], f1[0]], axis=2))
    f2 = forward(2, own2, near2, far2, end2, f1[1:])

    (end3, far3), near3, (f2, context_a), _ = step((end3, far3), near3, (f2, context_a))
    f3 = forward(3, own3, near3, far3, end3, f2[1:])

    late = []
    for t in range(n_dp):
        part = jnp.concatenate(
            [lax.dynamic_slice(f[0], (d ^ t, 0, 0), (1, rows, PAIR))[0] for f in (f2, f3)], axis=1
        )
        late.append(
            part if t == 0 else lax.ppermute(part, "dp", [(i, i ^ t) for i in range(n_dp)])
        )

    per_half = n_sec // n_mp
    span = half // per_half
    _, dkv, w = f3
    p_cols, q_own_cols, q_far_cols = (0, per_half), (1,), (per_half + 1,)
    pair = (2 * rows, 0)
    give_p = swap(backward(dkv, w, None, (2 * rows, 1), (span, p_cols), BF16))
    give_q = swap(backward(dkv, w, None, (2 * rows, 1), (span, q_far_cols + q_own_cols), BF16))
    send_y = backward(dkv, w, (give_p, 1, 0), (rows, 1), (span, p_cols), BF16)
    send_x = backward(dkv, w, (give_q, 0, 0), pair, (span, q_far_cols), BF16)
    send_y, send_x, late, dkv_, w_ = lax.optimization_barrier(
        (send_y, send_x, tuple(late), dkv, w)
    )
    got_y = lax.ppermute(send_y, "dp", ypairs)
    got_x = lax.ppermute(send_x, "mp", xpairs)
    p_own = backward(dkv_, w_, (give_p, 0, 0), (rows, 0), (span, p_cols), F32)
    q_own = backward(dkv_, w_, (give_q, 0, 1), pair, (span, q_own_cols), F32)
    context = gather_context(d, context_a, late)
    got_y, got_x, p_own, q_own, context = lax.optimization_barrier(
        (got_y, got_x, p_own, q_own, context)
    )
    to_x = (p_own[:, span:] + got_y[:, span:].astype(F32)).astype(BF16)
    to_y = (q_own[rows:] + got_x[rows:].astype(F32)).astype(BF16)
    last_x = lax.ppermute(to_x, "mp", xpairs)
    last_y = lax.ppermute(to_y, "dp", ypairs)
    enc_grad = finish(p_own, got_y, last_x, q_own, got_x, last_y)
    return (context, enc_grad)


def solution(mesh):
    placed = (
        P(("section", "dp"), "mp"),
        P(("section", "dp")),
        P(("section", "dp")),
        P(("section", "dp"), None),
        P(("section", "dp"), "mp"),
        P(("section", "dp"), "mp"),
        P(("section", "dp"), "mp"),
        P(("section", "dp"), "mp"),
    )
    sizes = tuple(mesh.shape[a] for a in ("section", "dp", "mp"))
    body = shards_section if sizes == (4, 4, 2) else shards_general
    return jax.shard_map(
        body,
        mesh=mesh,
        in_specs=placed,
        out_specs=(P(("section", "dp"), "mp"), P(("section", "dp"), "mp")),
        check_vma=False,
    )
```

```python
import functools

import jax
import jax.numpy as jnp
from jax import lax
from jax.experimental import pallas as pl
from jax.experimental.pallas import tpu as pltpu
from jax.sharding import PartitionSpec as P

DH = 64
BLOCK = 64
F32 = jnp.float32
BF16 = jnp.bfloat16


def attend(query_rows, key_rows, value_rows, grad_rows, key_lengths):
    block_count = key_lengths.shape[0]
    head_count = query_rows.shape[1] // DH
    shape_four = (block_count, BLOCK, head_count, DH)
    query_heads = query_rows.reshape(shape_four)
    key_heads = key_rows.reshape(shape_four)
    value_heads = value_rows.reshape(shape_four)
    grad_heads = grad_rows.reshape(shape_four)
    score_scale = DH ** (-0.5)
    scores = (
        jnp.einsum("bihd,bjhd->bhij", query_heads, key_heads, preferred_element_type=jnp.float32)
        * score_scale
    )
    visible = (
        jnp.arange(BLOCK, dtype=jnp.float32)[None, None, None, :] < key_lengths[:, None, None, None]
    )
    scores = jnp.where(visible, scores, -1e30)
    row_max = jnp.max(scores, axis=-1, keepdims=True)
    weights_exp = jnp.exp(scores - row_max)
    probabilities = weights_exp / jnp.sum(weights_exp, axis=-1, keepdims=True)
    prob_bf = probabilities.astype(jnp.bfloat16)
    context = jnp.einsum(
        "bhij,bjhd->bihd", prob_bf, value_heads, preferred_element_type=jnp.float32
    ).astype(jnp.bfloat16)
    prob_grad = jnp.einsum(
        "bihd,bjhd->bhij", grad_heads, value_heads, preferred_element_type=jnp.float32
    )
    row_dot = jnp.sum(probabilities * prob_grad, axis=-1, keepdims=True)
    score_grad = (probabilities * (prob_grad - row_dot) * score_scale).astype(jnp.bfloat16)
    key_grad = jnp.einsum(
        "bhij,bihd->bjhd", score_grad, query_heads, preferred_element_type=jnp.float32
    ).astype(jnp.bfloat16)
    value_grad = jnp.einsum(
        "bhij,bihd->bjhd", prob_bf, grad_heads, preferred_element_type=jnp.float32
    ).astype(jnp.bfloat16)
    flat_shape = (block_count * BLOCK, head_count * DH)
    return (
        context.reshape(flat_shape),
        key_grad.reshape(flat_shape),
        value_grad.reshape(flat_shape),
    )


def through(table, data, lead_shape):
    moved = jnp.dot(table, data, preferred_element_type=jnp.float32).astype(jnp.bfloat16)
    return moved.reshape(lead_shape + data.shape[1:])


def shards_general(enc_rows, enc_len, dest_dp, peer_counts, queries, ctx_grad, w_key, w_value):
    peer_count = lax.axis_size("dp")
    model_groups = lax.axis_size("mp")
    block_count = dest_dp.shape[0]
    slot_count = max(2, -(-block_count // peer_count))
    row_count, feature_width = enc_rows.shape
    key_full, value_full = (
        lax.all_gather(w_key, ("section", "dp"), axis=0, tiled=True),
        lax.all_gather(w_value, ("section", "dp"), axis=0, tiled=True),
    )
    positions = jnp.arange(block_count, dtype=jnp.int32)
    same_dest = dest_dp[:, None] == dest_dp[None, :]
    slot_rank = jnp.sum(
        (same_dest & (positions[None, :] < positions[:, None])).astype(jnp.int32), axis=1
    )
    target_slot = dest_dp * slot_count + slot_rank
    slot_ids = jnp.arange(peer_count * slot_count, dtype=jnp.int32)
    send_map = (slot_ids[:, None] == target_slot[None, :]).astype(jnp.bfloat16)
    arrivals = peer_counts[0]
    arrival_ends = jnp.cumsum(arrivals)
    sender = jnp.sum((arrival_ends[None, :] <= positions[:, None]).astype(jnp.int32), axis=1)
    first_pos = jnp.take(arrival_ends, sender) - jnp.take(arrivals, sender)
    slot_pick = sender * slot_count + positions - first_pos
    recv_map = (slot_pick[:, None] == slot_ids[None, :]).astype(jnp.bfloat16)
    lengths_own = enc_len.astype(jnp.float32).astype(jnp.bfloat16).reshape(block_count, 1)
    all_slots = peer_count * slot_count
    outgoing = through(send_map, enc_rows.reshape(block_count, -1), (peer_count, slot_count))
    outgoing_len = through(send_map, lengths_own, (peer_count, slot_count))
    incoming, incoming_len = (
        lax.all_to_all(outgoing, "dp", split_axis=0, concat_axis=0, tiled=True),
        lax.all_to_all(outgoing_len, "dp", split_axis=0, concat_axis=0, tiled=True),
    )
    rows_here = through(recv_map, incoming.reshape(all_slots, -1), (block_count,)).reshape(
        row_count, feature_width
    )
    lengths_here = through(recv_map, incoming_len.reshape(all_slots, 1), (block_count,))[
        :, 0
    ].astype(jnp.float32)
    shard_cols = lax.all_gather(rows_here, "mp", axis=1, tiled=True)
    key_acc = jnp.dot(shard_cols, key_full, preferred_element_type=jnp.float32)
    value_acc = jnp.dot(shard_cols, value_full, preferred_element_type=jnp.float32)
    context, key_grad, value_grad = attend(
        queries,
        key_acc.astype(jnp.bfloat16),
        value_acc.astype(jnp.bfloat16),
        ctx_grad,
        lengths_here,
    )
    col_span = key_full.shape[0] // model_groups
    pieces_out = []
    for group_idx in range(model_groups):
        key_part = key_full[group_idx * col_span : (group_idx + 1) * col_span]
        value_part = value_full[group_idx * col_span : (group_idx + 1) * col_span]
        partial_value = lax.dot_general(
            key_grad, key_part, (((1,), (1,)), ((), ())), preferred_element_type=jnp.float32
        )
        partial_value = partial_value + lax.dot_general(
            value_grad, value_part, (((1,), (1,)), ((), ())), preferred_element_type=jnp.float32
        )
        pieces_out.append(partial_value.astype(jnp.bfloat16))
    summed = lax.psum_scatter(
        jnp.concatenate(pieces_out, axis=1), "mp", scatter_dimension=1, tiled=True
    )
    outgoing_grad = through(recv_map.T, summed.reshape(block_count, -1), (peer_count, slot_count))
    returned = lax.all_to_all(outgoing_grad, "dp", split_axis=0, concat_axis=0, tiled=True)
    enc_grad = through(send_map.T, returned.reshape(all_slots, -1), (block_count,)).reshape(
        row_count, feature_width
    )
    return (context, enc_grad)


PAIR = 2 * DH
SLOTS = (0, 2, 1, 3)
VMEM = 56 << 20
SHORT = pl.CostEstimate(flops=1, bytes_accessed=1, transcendentals=0)


def nt(a, b):
    return lax.dot_general(a, b, (((1,), (1,)), ((), ())), preferred_element_type=F32)


def tn(a, b):
    return lax.dot_general(a, b, (((0,), (0,)), ((), ())), preferred_element_type=F32)


def forward_kernel(n_dp, n_sec, n_half, blk, in_slots, tab, *refs):
    blocks = n_dp * blk
    x_refs = refs[: n_half * n_dp]
    own, above, far, below, end = refs[n_half * n_dp : n_half * n_dp + 5]
    q_ref, g_ref = refs[n_half * n_dp + 5 : n_half * n_dp + 7]
    ctx_ref, dkv_ref, w_ref, acc, kv = refs[-5:]
    rows = acc.shape[0] // n_dp
    step = pl.program_id(0)
    per_half = n_sec // n_half
    z = tab[2 * blocks]
    m = tab[2 * blocks + 1]
    section = (m ^ (step // per_half)) * per_half + step % per_half
    hop = (section - z + n_sec) % n_sec

    def take(ref):
        if in_slots:
            d = tab[2 * blocks + 2]
            for t in range(n_dp):
                to = pl.multiple_of((d ^ t) * rows, rows)
                w_ref[pl.ds(to, rows), :] = ref[t * rows : (t + 1) * rows, :]
        else:
            w_ref[...] = ref[...].reshape(w_ref.shape)

    @pl.when(hop == 0)
    def _():
        take(own)

    @pl.when((hop == 1) & (z != n_sec - 1))
    def _():
        take(above)

    @pl.when(hop == 2)
    def _():
        take(far)

    @pl.when((hop == n_sec - 1) & (z != 0))
    def _():
        take(below)

    @pl.when(((hop == 1) & (z == n_sec - 1)) | ((hop == n_sec - 1) & (z == 0)))
    def _():
        take(end)

    for h in range(n_half):

        @pl.when(step // per_half == h)
        def _():
            for t in range(n_dp):
                at = slice(t * rows, (t + 1) * rows)
                part = jnp.dot(
                    x_refs[h * n_dp + t][0], w_ref[...], preferred_element_type=F32
                )
                if h == 0:
                    acc[at, :] = jnp.where(step == 0, part, acc[at, :] + part)
                else:
                    acc[at, :] += part

    @pl.when(step == n_sec - 1)
    def _():
        kv[...] = acc[...].astype(BF16)
        lane = lax.broadcasted_iota(jnp.int32, (BLOCK, PAIR), 1) < DH
        key_pos = lax.broadcasted_iota(jnp.int32, (BLOCK, PAIR), 0)
        scale = DH ** (-0.5)
        zero = jnp.zeros((BLOCK, PAIR), BF16)

        def group(bs):
            source = [pl.ds(pl.multiple_of(tab[b] * BLOCK, BLOCK), BLOCK) for b in bs]
            here = [pl.ds((b % blk) * BLOCK, BLOCK) for b in bs]
            key = [kv[at, 0:PAIR] for at in source]
            value = [kv[at, PAIR : 2 * PAIR] for at in source]

            def split(ref):
                rows_of = [ref[b // blk, at, :] for b, at in zip(bs, here)]
                return [
                    jnp.concatenate([jnp.where(lane, x, zero), jnp.where(lane, zero, x)], axis=0)
                    for x in rows_of
                ]

            query = split(q_ref)
            grad = split(g_ref)
            scores = [nt(k, q) * scale for k, q in zip(key, query)]
            prob_grad = [nt(v, g) for v, g in zip(value, grad)]
            scores = [jnp.where(key_pos < tab[blocks + b], x, -1e30) for b, x in zip(bs, scores)]
            weights = [jnp.exp(x - jnp.max(x, axis=0, keepdims=True)) for x in scores]
            probs = [x / jnp.sum(x, axis=0, keepdims=True) for x in weights]
            prob_bf = [x.astype(BF16) for x in probs]
            ctx = [tn(p, v) for p, v in zip(prob_bf, value)]
            dv = [jnp.dot(p, g, preferred_element_type=F32) for p, g in zip(prob_bf, grad)]
            row_dot = [jnp.sum(p * x, axis=0, keepdims=True) for p, x in zip(probs, prob_grad)]
            score_grad = [
                (p * (x - r) * scale).astype(BF16) for p, x, r in zip(probs, prob_grad, row_dot)
            ]
            dk = [jnp.dot(x, q, preferred_element_type=F32) for x, q in zip(score_grad, query)]
            for n, b in enumerate(bs):
                ctx_ref[b // blk, here[n], :] = jnp.where(
                    lane, ctx[n][:BLOCK], ctx[n][BLOCK:]
                ).astype(BF16)
                dkv_ref[source[n], 0:PAIR] = dk[n].astype(BF16)
                dkv_ref[source[n], PAIR : 2 * PAIR] = dv[n].astype(BF16)

        for b in range(0, blocks, blk):
            group(range(b, b + blk))


def forward_chunk(table, x, pieces, got, chunk, chunks, blk, n_sec, n_dp, before):
    n_half = x.shape[0] // n_dp
    cols = 2 * PAIR
    per_half = n_sec // n_half
    span = x.shape[2] // per_half
    rows = span // n_dp
    scalars = 2 * n_dp * blk

    def x_spec(h, slot):
        def at(a, t):
            sender = (t[scalars + 2] ^ slot) * n_half + (t[scalars + 1] ^ h)
            return (sender, 0, jnp.clip(a - h * per_half, 0, per_half - 1))

        return pl.BlockSpec((1, rows, span), at)

    def fixed(shape, at):
        return pl.BlockSpec(shape, lambda a, t: at)

    def head(at):
        return pl.BlockSpec((n_dp, rows, PAIR), lambda a, t: (0, 0, at))

    operands = [table] + [x] * (n_half * n_dp) + [p[0] for p in pieces] + [got, got]
    in_specs = [x_spec(h, slot) for h in range(n_half) for slot in SLOTS]
    in_specs += [fixed(shape, at) for _, shape, at in pieces]
    in_specs += [head(chunk), head(chunks + chunk)]
    aliases = {}
    if before is not None:
        aliases = {len(operands): 1, len(operands) + 1: 2}
        operands += before
        in_specs += [pl.BlockSpec(memory_space=pl.ANY)] * 2
    return pl.pallas_call(
        functools.partial(forward_kernel, n_dp, n_sec, n_half, blk, chunk == 0),
        grid_spec=pltpu.PrefetchScalarGridSpec(
            num_scalar_prefetch=1,
            grid=(n_sec,),
            in_specs=in_specs,
            out_specs=[
                head(0),
                pl.BlockSpec((n_dp * rows, cols), lambda a, t: (0, chunk)),
                pl.BlockSpec((span, cols), lambda a, t: (a, chunk)),
            ],
            scratch_shapes=[
                pltpu.VMEM((n_dp * rows, cols), F32),
                pltpu.VMEM((n_dp * rows, cols), BF16),
            ],
        ),
        out_shape=[
            jax.ShapeDtypeStruct((n_dp, rows, PAIR), BF16),
            jax.ShapeDtypeStruct((n_dp * rows, chunks * cols), BF16),
            jax.ShapeDtypeStruct((n_sec * span, chunks * cols), BF16),
        ],
        input_output_aliases=aliases,
        compiler_params=pltpu.CompilerParams(vmem_limit_bytes=VMEM),
        cost_estimate=SHORT,
        name="fwd",
    )(*operands)


def backward_kernel(*refs):
    depth = refs[0].shape[1]
    total = nt(refs[0][:, : 2 * PAIR], refs[1][:, : 2 * PAIR])
    for at in range(2 * PAIR, depth, 2 * PAIR):
        total += nt(refs[0][:, at : at + 2 * PAIR], refs[1][:, at : at + 2 * PAIR])
    for ref in refs[2:-1]:
        total += ref[...].astype(F32)
    refs[-1][...] = total.astype(refs[-1].dtype)


def backward(dkv, w, received, rows, cols, out_dtype):
    row_n, row_at = rows
    span, blocks = cols
    depth = dkv.shape[1]
    tile = 1024
    per_block = span // tile

    def col(i):
        at = blocks[0]
        for k in range(1, len(blocks)):
            at = jnp.where(i >= k * per_block, blocks[k], at)
        return at * per_block + i % per_block

    specs = [
        pl.BlockSpec((row_n, depth), lambda i: (row_at, 0)),
        pl.BlockSpec((tile, depth), lambda i: (col(i), 0)),
    ]
    extra = ()
    if received is not None:
        array, add_row, add_col = received
        specs.append(
            pl.BlockSpec((row_n, tile), lambda i: (add_row, add_col * per_block + i))
        )
        extra = (array,)
    return pl.pallas_call(
        backward_kernel,
        grid=(len(blocks) * per_block,),
        in_specs=specs,
        out_specs=pl.BlockSpec((row_n, tile), lambda i: (0, i)),
        out_shape=jax.ShapeDtypeStruct((row_n, len(blocks) * span), out_dtype),
        compiler_params=pltpu.CompilerParams(vmem_limit_bytes=VMEM),
        cost_estimate=SHORT,
        name="bwd",
    )(dkv, w, *extra)


def finish_kernel(p_ref, got_y, last_x, q_ref, got_x, last_y, out):
    span = out.shape[1] // 2
    out[:, :span] = (
        p_ref[...] + got_y[...].astype(F32) + last_x[...].astype(F32)
    ).astype(BF16)
    out[:, span:] = (
        q_ref[...] + got_x[...].astype(F32) + last_y[...].astype(F32)
    ).astype(BF16)


def finish(*operands):
    rows, span = operands[2].shape
    tiles = 2
    block = pl.BlockSpec((rows // tiles, span), lambda i: (i, 0))
    return pl.pallas_call(
        finish_kernel,
        grid=(tiles,),
        in_specs=[block] * 6,
        out_specs=pl.BlockSpec((rows // tiles, 2 * span), lambda i: (i, 0)),
        out_shape=jax.ShapeDtypeStruct((rows, 2 * span), BF16),
        compiler_params=pltpu.CompilerParams(vmem_limit_bytes=VMEM),
        cost_estimate=SHORT,
        name="finish",
    )(*operands)


def weight_kernel(k_ref, v_ref, out):
    out[0, :, :PAIR] = k_ref[...]
    out[0, :, PAIR:] = v_ref[...]


def pack_weights(w_key, w_value, chunk, n_dp):
    rows, width = w_key.shape
    per_owner = width // n_dp // PAIR
    block = pl.BlockSpec((rows, PAIR), lambda j: (0, j * per_owner + chunk))
    return pl.pallas_call(
        weight_kernel,
        grid=(n_dp,),
        in_specs=[block] * 2,
        out_specs=pl.BlockSpec((1, rows, 2 * PAIR), lambda j: (j, 0, 0)),
        out_shape=jax.ShapeDtypeStruct((n_dp, rows, 2 * PAIR), BF16),
        compiler_params=pltpu.CompilerParams(vmem_limit_bytes=VMEM),
        cost_estimate=SHORT,
        name="pack_weights",
    )(w_key, w_value)


def pack_kernel(q_ref, g_ref, k_ref, v_ref, small_ref, out):
    rows, cols = q_ref.shape
    parts = [q_ref[...], g_ref[...]]
    for c in range(0, k_ref.shape[1], PAIR):
        parts += [k_ref[:, c : c + PAIR], v_ref[:, c : c + PAIR]]
    at = 0
    for part in parts:
        out[0, :rows, at : at + part.shape[1]] = part
        at += part.shape[1]
    out[0, rows:, :] = jnp.zeros((out.shape[1] - rows, out.shape[2]), BF16)
    out[0, rows:, :PAIR] = small_ref[...]


def pack(queries, grads, w_key, w_value, small, n_dp):
    rows, width = queries.shape
    cols = width // n_dp
    block = pl.BlockSpec((rows, cols), lambda j: (0, j))
    tail = pl.BlockSpec((rows, cols // 2), lambda j: (0, 2 * j + 1))
    extra = small.shape[0]
    return pl.pallas_call(
        pack_kernel,
        grid=(n_dp,),
        in_specs=[block, block, tail, tail, pl.BlockSpec(small.shape, lambda j: (0, 0))],
        out_specs=pl.BlockSpec((1, rows + extra, 3 * cols), lambda j: (j, 0, 0)),
        out_shape=jax.ShapeDtypeStruct((n_dp, rows + extra, 3 * cols), BF16),
        compiler_params=pltpu.CompilerParams(vmem_limit_bytes=VMEM),
        cost_estimate=SHORT,
        name="pack",
    )(queries, grads, w_key, w_value, small)


def context_kernel(n_dp, tab, early, *refs):
    out = refs[-1]
    cols = early.shape[2]
    out[:, :cols] = early[0]
    for t in range(n_dp):

        @pl.when(pl.program_id(0) == t)
        def _():
            out[:, cols:] = refs[t][...]


def gather_context(d, early, late):
    n_dp, rows, cols = early.shape
    last = late[0].shape[1]
    return pl.pallas_call(
        functools.partial(context_kernel, n_dp),
        grid_spec=pltpu.PrefetchScalarGridSpec(
            num_scalar_prefetch=1,
            grid=(n_dp,),
            in_specs=[pl.BlockSpec((1, rows, cols), lambda t, tab: (tab[0] ^ t, 0, 0))]
            + [pl.BlockSpec((rows, last), lambda t, tab: (0, 0))] * n_dp,
            out_specs=pl.BlockSpec((rows, cols + last), lambda t, tab: (0, tab[0] ^ t)),
        ),
        out_shape=jax.ShapeDtypeStruct((rows, n_dp * (cols + last)), BF16),
        compiler_params=pltpu.CompilerParams(vmem_limit_bytes=VMEM),
        cost_estimate=SHORT,
        name="gather_context",
    )(d.reshape(1), early, *late)


def shards_section(enc_rows, enc_len, dest_dp, peer_counts, queries, ctx_grad, w_key, w_value):
    n_sec, n_dp, n_mp = (lax.axis_size(a) for a in ("section", "dp", "mp"))
    z, d, m = (lax.axis_index(a).astype(jnp.int32) for a in ("section", "dp", "mp"))
    blk = dest_dp.shape[0]
    blocks = blk * n_dp
    rows, half = enc_rows.shape
    head_cols = w_key.shape[1] // n_dp

    core = [(i, i ^ 1) for i in range(n_dp)]
    ypairs = [(i, i ^ 2) for i in range(n_dp)]
    xpairs = [(0, 1), (1, 0)]
    up = [(i, i + 1) for i in range(n_sec - 1)]
    down = [(i + 1, i) for i in range(n_sec - 1)]
    over_two = [(i, i ^ 2) for i in range(n_sec)]
    ends = [(1, 0), (2, 3)]
    outer = [(0, n_sec - 1), (n_sec - 1, 0)]

    def step(*waited, released=()):
        done = ()
        for group in waited:
            done = done + (tuple(group),)
            if group is not waited[-1]:
                done = lax.optimization_barrier(done)
        done, released = lax.optimization_barrier((done, tuple(released)))
        return (*done, released)

    def swap(x):
        return lax.ppermute(x, "dp", core)

    def exchange(x):
        return lax.all_to_all(x, "dp", split_axis=0, concat_axis=0, tiled=True)

    def sides(piece):
        return lax.ppermute(piece, "section", up), lax.ppermute(piece, "section", down)

    def beyond(piece):
        return lax.ppermute(piece, "section", over_two)

    def turn(far):
        return lax.ppermute(far, "section", ends)

    def flat(x):
        return x.reshape(n_dp * rows, 2 * PAIR)

    pieces = []
    for t in range(n_dp):
        at = (d ^ t) * head_cols
        cut = jnp.concatenate(
            [lax.dynamic_slice(w, (0, at), (rows, PAIR)) for w in (w_key, w_value)], axis=1
        )
        pieces.append(cut if t == 0 else lax.ppermute(cut, "dp", [(i, i ^ t) for i in range(n_dp)]))
    own0 = jnp.concatenate(pieces, axis=0)
    x = lax.all_gather(enc_rows, ("dp", "mp"), axis=0, tiled=False)
    small = jnp.concatenate([enc_len, dest_dp, peer_counts[0]]).astype(BF16)
    small = jnp.pad(small[None, :], ((0, 15), (0, PAIR - small.shape[0])))

    (own0,), (w_k, w_v) = step((own0,), released=(w_key, w_value))
    near0, far0 = sides(own0), beyond(own0)
    own1 = flat(exchange(pack_weights(w_k, w_v, 1, n_dp)))
    parts = pack(queries, ctx_grad, w_k, w_v, small, n_dp)

    (far0,), near0, (own1, parts), _ = step((far0,), near0, (own1, parts))
    near1, far1, end0 = sides(own1), beyond(own1), turn(far0)
    got = exchange(parts)

    (end0,), (far1,), near1, (x, got), _ = step((end0,), (far1,), near1, (x, got))
    own2, own3 = (
        flat(got[:, :rows, 2 * head_cols + 2 * PAIR * i : 2 * head_cols + 2 * PAIR * (i + 1)])
        for i in range(2)
    )
    near2, far2, end1 = sides(own2), beyond(own2), turn(far1)

    packs = got[:, rows, : 2 * blk + n_dp].astype(jnp.int32)
    lens = packs[:, :blk].reshape(-1)
    dest = packs[:, blk : 2 * blk]
    counts = packs[:, 2 * blk :]
    peer = jnp.arange(n_dp, dtype=jnp.int32)
    pos = jnp.arange(blk, dtype=jnp.int32)
    before = jnp.sum(
        jnp.where(peer[None, None, :] < peer[None, :, None], counts[:, None, :], 0), axis=2
    )
    upto = before + counts
    sender = jnp.sum((upto[:, None, :] <= pos[None, :, None]).astype(jnp.int32), axis=2)
    is_sender = sender[:, :, None] == peer[None, None, :]
    rank = pos[None, :] - jnp.sum(jnp.where(is_sender, before[:, None, :], 0), axis=2)
    same = dest[:, :, None] == dest[:, None, :]
    slot_rank = jnp.sum((same & (pos[None, None, :] < pos[None, :, None])).astype(jnp.int32), axis=2)
    hit = (
        is_sender[:, :, :, None]
        & (dest[None, None] == peer[:, None, None, None])
        & (slot_rank[None, None] == rank[:, :, None, None])
    ).reshape(blocks, blocks)
    gap = peer ^ d
    gap = jnp.where(gap == 1, 2, jnp.where(gap == 2, 1, gap))
    place = (gap[:, None] * blk + pos[None, :]).reshape(-1)
    src = jnp.sum(jnp.where(hit, place[None, :], 0), axis=1)
    src_len = jnp.sum(jnp.where(hit, lens[None, :], 0), axis=1)
    table = jnp.concatenate([src, src_len, jnp.stack([z, m, d])])

    chunks = head_cols // PAIR

    def forward(c, own, near, far, end, before):
        pieces = [(x, x.shape, (0, 0)) for x in (own, near[1], far, near[0], end)]
        return forward_chunk(
            table, x, pieces, got, c, chunks, blk, n_sec, n_dp, before
        )

    f0 = forward(0, own0, near0, far0, end0, None)

    (end1,), (far2,), near2, (own3, f0), _ = step((end1,), (far2,), near2, (own3, f0))
    far3, end2 = beyond(own3), turn(far2)
    end3 = lax.ppermute(own3, "section", outer)
    f1 = forward(1, own1, near1, far1, end1, f0[1:])
    f1, own3_ = lax.optimization_barrier((f1, own3))
    near3 = sides(own3_)
    context_a = exchange(jnp.concatenate([f0[0], f1[0]], axis=2))
    f2 = forward(2, own2, near2, far2, end2, f1[1:])

    (end3, far3), near3, (f2, context_a), _ = step((end3, far3), near3, (f2, context_a))
    f3 = forward(3, own3, near3, far3, end3, f2[1:])

    late = []
    for t in range(n_dp):
        part = jnp.concatenate(
            [lax.dynamic_slice(f[0], (d ^ t, 0, 0), (1, rows, PAIR))[0] for f in (f2, f3)], axis=1
        )
        late.append(
            part if t == 0 else lax.ppermute(part, "dp", [(i, i ^ t) for i in range(n_dp)])
        )

    per_half = n_sec // n_mp
    span = half // per_half
    _, dkv, w = f3
    p_cols, q_own_cols, q_far_cols = (0, per_half), (1,), (per_half + 1,)
    pair = (2 * rows, 0)
    give_p = swap(backward(dkv, w, None, (2 * rows, 1), (span, p_cols), BF16))
    give_q = swap(backward(dkv, w, None, (2 * rows, 1), (span, q_far_cols + q_own_cols), BF16))
    send_y = backward(dkv, w, (give_p, 1, 0), (rows, 1), (span, p_cols), BF16)
    send_x = backward(dkv, w, (give_q, 0, 0), pair, (span, q_far_cols), BF16)
    send_y, send_x, late, dkv_, w_ = lax.optimization_barrier(
        (send_y, send_x, tuple(late), dkv, w)
    )
    got_y = lax.ppermute(send_y, "dp", ypairs)
    got_x = lax.ppermute(send_x, "mp", xpairs)
    p_own = backward(dkv_, w_, (give_p, 0, 0), (rows, 0), (span, p_cols), F32)
    q_own = backward(dkv_, w_, (give_q, 0, 1), pair, (span, q_own_cols), F32)
    context = gather_context(d, context_a, late)
    got_y, got_x, p_own, q_own, context = lax.optimization_barrier(
        (got_y, got_x, p_own, q_own, context)
    )
    to_x = (p_own[:, span:] + got_y[:, span:].astype(F32)).astype(BF16)
    to_y = (q_own[rows:] + got_x[rows:].astype(F32)).astype(BF16)
    last_x = lax.ppermute(to_x, "mp", xpairs)
    last_y = lax.ppermute(to_y, "dp", ypairs)
    enc_grad = finish(p_own, got_y, last_x, q_own, got_x, last_y)
    return (context, enc_grad)


def solution(mesh):
    placed = (
        P(("section", "dp"), "mp"),
        P(("section", "dp")),
        P(("section", "dp")),
        P(("section", "dp"), None),
        P(("section", "dp"), "mp"),
        P(("section", "dp"), "mp"),
        P(("section", "dp"), "mp"),
        P(("section", "dp"), "mp"),
    )
    sizes = tuple(mesh.shape[a] for a in ("section", "dp", "mp"))
    body = shards_section if sizes == (4, 4, 2) else shards_general
    return jax.shard_map(
        body,
        mesh=mesh,
        in_specs=placed,
        out_specs=(P(("section", "dp"), "mp"), P(("section", "dp"), "mp")),
        check_vma=False,
    )
```

```python
import functools

import jax
import jax.numpy as jnp
from jax import lax
from jax.experimental import pallas as pl
from jax.experimental.pallas import tpu as pltpu
from jax.sharding import PartitionSpec as P

DH = 64
BLOCK = 64
F32 = jnp.float32
BF16 = jnp.bfloat16


def attend(query_rows, key_rows, value_rows, grad_rows, key_lengths):
    block_count = key_lengths.shape[0]
    head_count = query_rows.shape[1] // DH
    shape_four = (block_count, BLOCK, head_count, DH)
    query_heads = query_rows.reshape(shape_four)
    key_heads = key_rows.reshape(shape_four)
    value_heads = value_rows.reshape(shape_four)
    grad_heads = grad_rows.reshape(shape_four)
    score_scale = DH ** (-0.5)
    scores = (
        jnp.einsum("bihd,bjhd->bhij", query_heads, key_heads, preferred_element_type=jnp.float32)
        * score_scale
    )
    visible = (
        jnp.arange(BLOCK, dtype=jnp.float32)[None, None, None, :] < key_lengths[:, None, None, None]
    )
    scores = jnp.where(visible, scores, -1e30)
    row_max = jnp.max(scores, axis=-1, keepdims=True)
    weights_exp = jnp.exp(scores - row_max)
    probabilities = weights_exp / jnp.sum(weights_exp, axis=-1, keepdims=True)
    prob_bf = probabilities.astype(jnp.bfloat16)
    context = jnp.einsum(
        "bhij,bjhd->bihd", prob_bf, value_heads, preferred_element_type=jnp.float32
    ).astype(jnp.bfloat16)
    prob_grad = jnp.einsum(
        "bihd,bjhd->bhij", grad_heads, value_heads, preferred_element_type=jnp.float32
    )
    row_dot = jnp.sum(probabilities * prob_grad, axis=-1, keepdims=True)
    score_grad = (probabilities * (prob_grad - row_dot) * score_scale).astype(jnp.bfloat16)
    key_grad = jnp.einsum(
        "bhij,bihd->bjhd", score_grad, query_heads, preferred_element_type=jnp.float32
    ).astype(jnp.bfloat16)
    value_grad = jnp.einsum(
        "bhij,bihd->bjhd", prob_bf, grad_heads, preferred_element_type=jnp.float32
    ).astype(jnp.bfloat16)
    flat_shape = (block_count * BLOCK, head_count * DH)
    return (
        context.reshape(flat_shape),
        key_grad.reshape(flat_shape),
        value_grad.reshape(flat_shape),
    )


def through(table, data, lead_shape):
    moved = jnp.dot(table, data, preferred_element_type=jnp.float32).astype(jnp.bfloat16)
    return moved.reshape(lead_shape + data.shape[1:])


def shards_general(enc_rows, enc_len, dest_dp, peer_counts, queries, ctx_grad, w_key, w_value):
    peer_count = lax.axis_size("dp")
    model_groups = lax.axis_size("mp")
    block_count = dest_dp.shape[0]
    slot_count = max(2, -(-block_count // peer_count))
    row_count, feature_width = enc_rows.shape
    key_full, value_full = (
        lax.all_gather(w_key, ("section", "dp"), axis=0, tiled=True),
        lax.all_gather(w_value, ("section", "dp"), axis=0, tiled=True),
    )
    positions = jnp.arange(block_count, dtype=jnp.int32)
    same_dest = dest_dp[:, None] == dest_dp[None, :]
    slot_rank = jnp.sum(
        (same_dest & (positions[None, :] < positions[:, None])).astype(jnp.int32), axis=1
    )
    target_slot = dest_dp * slot_count + slot_rank
    slot_ids = jnp.arange(peer_count * slot_count, dtype=jnp.int32)
    send_map = (slot_ids[:, None] == target_slot[None, :]).astype(jnp.bfloat16)
    arrivals = peer_counts[0]
    arrival_ends = jnp.cumsum(arrivals)
    sender = jnp.sum((arrival_ends[None, :] <= positions[:, None]).astype(jnp.int32), axis=1)
    first_pos = jnp.take(arrival_ends, sender) - jnp.take(arrivals, sender)
    slot_pick = sender * slot_count + positions - first_pos
    recv_map = (slot_pick[:, None] == slot_ids[None, :]).astype(jnp.bfloat16)
    lengths_own = enc_len.astype(jnp.float32).astype(jnp.bfloat16).reshape(block_count, 1)
    all_slots = peer_count * slot_count
    outgoing = through(send_map, enc_rows.reshape(block_count, -1), (peer_count, slot_count))
    outgoing_len = through(send_map, lengths_own, (peer_count, slot_count))
    incoming, incoming_len = (
        lax.all_to_all(outgoing, "dp", split_axis=0, concat_axis=0, tiled=True),
        lax.all_to_all(outgoing_len, "dp", split_axis=0, concat_axis=0, tiled=True),
    )
    rows_here = through(recv_map, incoming.reshape(all_slots, -1), (block_count,)).reshape(
        row_count, feature_width
    )
    lengths_here = through(recv_map, incoming_len.reshape(all_slots, 1), (block_count,))[
        :, 0
    ].astype(jnp.float32)
    shard_cols = lax.all_gather(rows_here, "mp", axis=1, tiled=True)
    key_acc = jnp.dot(shard_cols, key_full, preferred_element_type=jnp.float32)
    value_acc = jnp.dot(shard_cols, value_full, preferred_element_type=jnp.float32)
    context, key_grad, value_grad = attend(
        queries,
        key_acc.astype(jnp.bfloat16),
        value_acc.astype(jnp.bfloat16),
        ctx_grad,
        lengths_here,
    )
    col_span = key_full.shape[0] // model_groups
    pieces_out = []
    for group_idx in range(model_groups):
        key_part = key_full[group_idx * col_span : (group_idx + 1) * col_span]
        value_part = value_full[group_idx * col_span : (group_idx + 1) * col_span]
        partial_value = lax.dot_general(
            key_grad, key_part, (((1,), (1,)), ((), ())), preferred_element_type=jnp.float32
        )
        partial_value = partial_value + lax.dot_general(
            value_grad, value_part, (((1,), (1,)), ((), ())), preferred_element_type=jnp.float32
        )
        pieces_out.append(partial_value.astype(jnp.bfloat16))
    summed = lax.psum_scatter(
        jnp.concatenate(pieces_out, axis=1), "mp", scatter_dimension=1, tiled=True
    )
    outgoing_grad = through(recv_map.T, summed.reshape(block_count, -1), (peer_count, slot_count))
    returned = lax.all_to_all(outgoing_grad, "dp", split_axis=0, concat_axis=0, tiled=True)
    enc_grad = through(send_map.T, returned.reshape(all_slots, -1), (block_count,)).reshape(
        row_count, feature_width
    )
    return (context, enc_grad)


PAIR = 2 * DH
SLOTS = (0, 2, 1, 3)
VMEM = 56 << 20
SHORT = pl.CostEstimate(flops=1, bytes_accessed=1, transcendentals=0)


def nt(a, b):
    return lax.dot_general(a, b, (((1,), (1,)), ((), ())), preferred_element_type=F32)


def tn(a, b):
    return lax.dot_general(a, b, (((0,), (0,)), ((), ())), preferred_element_type=F32)


def forward_kernel(n_dp, n_sec, n_half, blk, in_slots, tab, *refs):
    blocks = n_dp * blk
    x_refs = refs[: n_half * n_dp]
    own, above, far, below, end = refs[n_half * n_dp : n_half * n_dp + 5]
    q_ref, g_ref = refs[n_half * n_dp + 5 : n_half * n_dp + 7]
    ctx_ref, dkv_ref, w_ref, acc, kv = refs[-5:]
    rows = acc.shape[0] // n_dp
    step = pl.program_id(0)
    per_half = n_sec // n_half
    z = tab[2 * blocks]
    m = tab[2 * blocks + 1]
    section = (m ^ (step // per_half)) * per_half + step % per_half
    hop = (section - z + n_sec) % n_sec

    def take(ref):
        if in_slots:
            d = tab[2 * blocks + 2]
            for t in range(n_dp):
                to = pl.multiple_of((d ^ t) * rows, rows)
                w_ref[pl.ds(to, rows), :] = ref[t * rows : (t + 1) * rows, :]
        else:
            w_ref[...] = ref[...].reshape(w_ref.shape)

    @pl.when(hop == 0)
    def _():
        take(own)

    @pl.when((hop == 1) & (z != n_sec - 1))
    def _():
        take(above)

    @pl.when(hop == 2)
    def _():
        take(far)

    @pl.when((hop == n_sec - 1) & (z != 0))
    def _():
        take(below)

    @pl.when(((hop == 1) & (z == n_sec - 1)) | ((hop == n_sec - 1) & (z == 0)))
    def _():
        take(end)

    for h in range(n_half):

        @pl.when(step // per_half == h)
        def _():
            for t in range(n_dp):
                at = slice(t * rows, (t + 1) * rows)
                part = jnp.dot(
                    x_refs[h * n_dp + t][0], w_ref[...], preferred_element_type=F32
                )
                if h == 0:
                    acc[at, :] = jnp.where(step == 0, part, acc[at, :] + part)
                else:
                    acc[at, :] += part

    @pl.when(step == n_sec - 1)
    def _():
        kv[...] = acc[...].astype(BF16)
        lane = lax.broadcasted_iota(jnp.int32, (BLOCK, PAIR), 1) < DH
        key_pos = lax.broadcasted_iota(jnp.int32, (BLOCK, PAIR), 0)
        scale = DH ** (-0.5)
        zero = jnp.zeros((BLOCK, PAIR), BF16)

        def group(bs):
            source = [pl.ds(pl.multiple_of(tab[b] * BLOCK, BLOCK), BLOCK) for b in bs]
            here = [pl.ds((b % blk) * BLOCK, BLOCK) for b in bs]
            key = [kv[at, 0:PAIR] for at in source]
            value = [kv[at, PAIR : 2 * PAIR] for at in source]

            def split(ref):
                rows_of = [ref[b // blk, at, :] for b, at in zip(bs, here)]
                return [
                    jnp.concatenate([jnp.where(lane, x, zero), jnp.where(lane, zero, x)], axis=0)
                    for x in rows_of
                ]

            query = split(q_ref)
            grad = split(g_ref)
            scores = [nt(k, q) * scale for k, q in zip(key, query)]
            prob_grad = [nt(v, g) for v, g in zip(value, grad)]
            scores = [jnp.where(key_pos < tab[blocks + b], x, -1e30) for b, x in zip(bs, scores)]
            weights = [jnp.exp(x - jnp.max(x, axis=0, keepdims=True)) for x in scores]
            probs = [x / jnp.sum(x, axis=0, keepdims=True) for x in weights]
            prob_bf = [x.astype(BF16) for x in probs]
            ctx = [tn(p, v) for p, v in zip(prob_bf, value)]
            dv = [jnp.dot(p, g, preferred_element_type=F32) for p, g in zip(prob_bf, grad)]
            row_dot = [jnp.sum(p * x, axis=0, keepdims=True) for p, x in zip(probs, prob_grad)]
            score_grad = [
                (p * (x - r) * scale).astype(BF16) for p, x, r in zip(probs, prob_grad, row_dot)
            ]
            dk = [jnp.dot(x, q, preferred_element_type=F32) for x, q in zip(score_grad, query)]
            for n, b in enumerate(bs):
                ctx_ref[b // blk, here[n], :] = jnp.where(
                    lane, ctx[n][:BLOCK], ctx[n][BLOCK:]
                ).astype(BF16)
                dkv_ref[source[n], 0:PAIR] = dk[n].astype(BF16)
                dkv_ref[source[n], PAIR : 2 * PAIR] = dv[n].astype(BF16)

        for b in range(0, blocks, blk):
            group(range(b, b + blk))


def forward_chunk(table, x, pieces, got, chunk, chunks, blk, n_sec, n_dp, before):
    n_half = x.shape[0] // n_dp
    cols = 2 * PAIR
    per_half = n_sec // n_half
    span = x.shape[2] // per_half
    rows = span // n_dp
    scalars = 2 * n_dp * blk

    def x_spec(h, slot):
        def at(a, t):
            sender = (t[scalars + 2] ^ slot) * n_half + (t[scalars + 1] ^ h)
            return (sender, 0, jnp.clip(a - h * per_half, 0, per_half - 1))

        return pl.BlockSpec((1, rows, span), at)

    def fixed(shape, at):
        return pl.BlockSpec(shape, lambda a, t: at)

    def head(at):
        return pl.BlockSpec((n_dp, rows, PAIR), lambda a, t: (0, 0, at))

    operands = [table] + [x] * (n_half * n_dp) + [p[0] for p in pieces] + [got, got]
    in_specs = [x_spec(h, slot) for h in range(n_half) for slot in SLOTS]
    in_specs += [fixed(shape, at) for _, shape, at in pieces]
    in_specs += [head(chunk), head(chunks + chunk)]
    aliases = {}
    if before is not None:
        aliases = {len(operands): 1, len(operands) + 1: 2}
        operands += before
        in_specs += [pl.BlockSpec(memory_space=pl.ANY)] * 2
    return pl.pallas_call(
        functools.partial(forward_kernel, n_dp, n_sec, n_half, blk, chunk == 0),
        grid_spec=pltpu.PrefetchScalarGridSpec(
            num_scalar_prefetch=1,
            grid=(n_sec,),
            in_specs=in_specs,
            out_specs=[
                head(0),
                pl.BlockSpec((n_dp * rows, cols), lambda a, t: (0, chunk)),
                pl.BlockSpec((span, cols), lambda a, t: (a, chunk)),
            ],
            scratch_shapes=[
                pltpu.VMEM((n_dp * rows, cols), F32),
                pltpu.VMEM((n_dp * rows, cols), BF16),
            ],
        ),
        out_shape=[
            jax.ShapeDtypeStruct((n_dp, rows, PAIR), BF16),
            jax.ShapeDtypeStruct((n_dp * rows, chunks * cols), BF16),
            jax.ShapeDtypeStruct((n_sec * span, chunks * cols), BF16),
        ],
        input_output_aliases=aliases,
        compiler_params=pltpu.CompilerParams(vmem_limit_bytes=VMEM),
        cost_estimate=SHORT,
        name="fwd",
    )(*operands)


def backward_kernel(*refs):
    depth = refs[0].shape[1]
    total = nt(refs[0][:, : 2 * PAIR], refs[1][:, : 2 * PAIR])
    for at in range(2 * PAIR, depth, 2 * PAIR):
        total += nt(refs[0][:, at : at + 2 * PAIR], refs[1][:, at : at + 2 * PAIR])
    for ref in refs[2:-1]:
        total += ref[...].astype(F32)
    refs[-1][...] = total.astype(refs[-1].dtype)


def backward(dkv, w, received, rows, cols, out_dtype):
    row_n, row_at = rows
    span, blocks = cols
    depth = dkv.shape[1]
    tile = 1024
    per_block = span // tile

    def col(i):
        at = blocks[0]
        for k in range(1, len(blocks)):
            at = jnp.where(i >= k * per_block, blocks[k], at)
        return at * per_block + i % per_block

    specs = [
        pl.BlockSpec((row_n, depth), lambda i: (row_at, 0)),
        pl.BlockSpec((tile, depth), lambda i: (col(i), 0)),
    ]
    extra = ()
    if received is not None:
        array, add_row, add_col = received
        specs.append(
            pl.BlockSpec((row_n, tile), lambda i: (add_row, add_col * per_block + i))
        )
        extra = (array,)
    return pl.pallas_call(
        backward_kernel,
        grid=(len(blocks) * per_block,),
        in_specs=specs,
        out_specs=pl.BlockSpec((row_n, tile), lambda i: (0, i)),
        out_shape=jax.ShapeDtypeStruct((row_n, len(blocks) * span), out_dtype),
        compiler_params=pltpu.CompilerParams(vmem_limit_bytes=VMEM),
        cost_estimate=SHORT,
        name="bwd",
    )(dkv, w, *extra)


def finish_kernel(p_ref, got_y, last_x, q_ref, got_x, last_y, out):
    span = out.shape[1] // 2
    out[:, :span] = (
        p_ref[...] + got_y[...].astype(F32) + last_x[...].astype(F32)
    ).astype(BF16)
    out[:, span:] = (
        q_ref[...] + got_x[...].astype(F32) + last_y[...].astype(F32)
    ).astype(BF16)


def finish(*operands):
    rows, span = operands[2].shape
    tiles = 2
    block = pl.BlockSpec((rows // tiles, span), lambda i: (i, 0))
    return pl.pallas_call(
        finish_kernel,
        grid=(tiles,),
        in_specs=[block] * 6,
        out_specs=pl.BlockSpec((rows // tiles, 2 * span), lambda i: (i, 0)),
        out_shape=jax.ShapeDtypeStruct((rows, 2 * span), BF16),
        compiler_params=pltpu.CompilerParams(vmem_limit_bytes=16 << 20),
        cost_estimate=SHORT,
        name="finish",
    )(*operands)


def weight_kernel(k_ref, v_ref, out):
    out[0, :, :PAIR] = k_ref[...]
    out[0, :, PAIR:] = v_ref[...]


def pack_weights(w_key, w_value, chunk, n_dp):
    rows, width = w_key.shape
    per_owner = width // n_dp // PAIR
    block = pl.BlockSpec((rows, PAIR), lambda j: (0, j * per_owner + chunk))
    return pl.pallas_call(
        weight_kernel,
        grid=(n_dp,),
        in_specs=[block] * 2,
        out_specs=pl.BlockSpec((1, rows, 2 * PAIR), lambda j: (j, 0, 0)),
        out_shape=jax.ShapeDtypeStruct((n_dp, rows, 2 * PAIR), BF16),
        compiler_params=pltpu.CompilerParams(vmem_limit_bytes=VMEM),
        cost_estimate=SHORT,
        name="pack_weights",
    )(w_key, w_value)


def pack_kernel(q_ref, g_ref, k_ref, v_ref, small_ref, out):
    rows, cols = q_ref.shape
    parts = [q_ref[...], g_ref[...]]
    for c in range(0, k_ref.shape[1], PAIR):
        parts += [k_ref[:, c : c + PAIR], v_ref[:, c : c + PAIR]]
    at = 0
    for part in parts:
        out[0, :rows, at : at + part.shape[1]] = part
        at += part.shape[1]
    out[0, rows:, :] = jnp.zeros((out.shape[1] - rows, out.shape[2]), BF16)
    out[0, rows:, :PAIR] = small_ref[...]


def pack(queries, grads, w_key, w_value, small, n_dp):
    rows, width = queries.shape
    cols = width // n_dp
    block = pl.BlockSpec((rows, cols), lambda j: (0, j))
    tail = pl.BlockSpec((rows, cols // 2), lambda j: (0, 2 * j + 1))
    extra = small.shape[0]
    return pl.pallas_call(
        pack_kernel,
        grid=(n_dp,),
        in_specs=[block, block, tail, tail, pl.BlockSpec(small.shape, lambda j: (0, 0))],
        out_specs=pl.BlockSpec((1, rows + extra, 3 * cols), lambda j: (j, 0, 0)),
        out_shape=jax.ShapeDtypeStruct((n_dp, rows + extra, 3 * cols), BF16),
        compiler_params=pltpu.CompilerParams(vmem_limit_bytes=VMEM),
        cost_estimate=SHORT,
        name="pack",
    )(queries, grads, w_key, w_value, small)


def context_kernel(n_dp, tab, early, *refs):
    out = refs[-1]
    cols = early.shape[2]
    out[:, :cols] = early[0]
    for t in range(n_dp):

        @pl.when(pl.program_id(0) == t)
        def _():
            out[:, cols:] = refs[t][...]


def gather_context(d, early, late):
    n_dp, rows, cols = early.shape
    last = late[0].shape[1]
    return pl.pallas_call(
        functools.partial(context_kernel, n_dp),
        grid_spec=pltpu.PrefetchScalarGridSpec(
            num_scalar_prefetch=1,
            grid=(n_dp,),
            in_specs=[pl.BlockSpec((1, rows, cols), lambda t, tab: (tab[0] ^ t, 0, 0))]
            + [pl.BlockSpec((rows, last), lambda t, tab: (0, 0))] * n_dp,
            out_specs=pl.BlockSpec((rows, cols + last), lambda t, tab: (0, tab[0] ^ t)),
        ),
        out_shape=jax.ShapeDtypeStruct((rows, n_dp * (cols + last)), BF16),
        compiler_params=pltpu.CompilerParams(vmem_limit_bytes=VMEM),
        cost_estimate=SHORT,
        name="gather_context",
    )(d.reshape(1), early, *late)


def shards_section(enc_rows, enc_len, dest_dp, peer_counts, queries, ctx_grad, w_key, w_value):
    n_sec, n_dp, n_mp = (lax.axis_size(a) for a in ("section", "dp", "mp"))
    z, d, m = (lax.axis_index(a).astype(jnp.int32) for a in ("section", "dp", "mp"))
    blk = dest_dp.shape[0]
    blocks = blk * n_dp
    rows, half = enc_rows.shape
    head_cols = w_key.shape[1] // n_dp

    core = [(i, i ^ 1) for i in range(n_dp)]
    ypairs = [(i, i ^ 2) for i in range(n_dp)]
    xpairs = [(0, 1), (1, 0)]
    up = [(i, i + 1) for i in range(n_sec - 1)]
    down = [(i + 1, i) for i in range(n_sec - 1)]
    over_two = [(i, i ^ 2) for i in range(n_sec)]
    ends = [(1, 0), (2, 3)]
    outer = [(0, n_sec - 1), (n_sec - 1, 0)]

    def step(*waited, released=()):
        done = ()
        for group in waited:
            done = done + (tuple(group),)
            if group is not waited[-1]:
                done = lax.optimization_barrier(done)
        done, released = lax.optimization_barrier((done, tuple(released)))
        return (*done, released)

    def swap(x):
        return lax.ppermute(x, "dp", core)

    def exchange(x):
        return lax.all_to_all(x, "dp", split_axis=0, concat_axis=0, tiled=True)

    def sides(piece):
        return lax.ppermute(piece, "section", up), lax.ppermute(piece, "section", down)

    def beyond(piece):
        return lax.ppermute(piece, "section", over_two)

    def turn(far):
        return lax.ppermute(far, "section", ends)

    def flat(x):
        return x.reshape(n_dp * rows, 2 * PAIR)

    pieces = []
    for t in range(n_dp):
        at = (d ^ t) * head_cols
        cut = jnp.concatenate(
            [lax.dynamic_slice(w, (0, at), (rows, PAIR)) for w in (w_key, w_value)], axis=1
        )
        pieces.append(cut if t == 0 else lax.ppermute(cut, "dp", [(i, i ^ t) for i in range(n_dp)]))
    own0 = jnp.concatenate(pieces, axis=0)
    x = lax.all_gather(enc_rows, ("dp", "mp"), axis=0, tiled=False)
    small = jnp.concatenate([enc_len, dest_dp, peer_counts[0]]).astype(BF16)
    small = jnp.pad(small[None, :], ((0, 15), (0, PAIR - small.shape[0])))

    (own0,), (w_k, w_v) = step((own0,), released=(w_key, w_value))
    near0, far0 = sides(own0), beyond(own0)
    own1 = flat(exchange(pack_weights(w_k, w_v, 1, n_dp)))
    parts = pack(queries, ctx_grad, w_k, w_v, small, n_dp)

    (far0,), near0, (own1, parts), _ = step((far0,), near0, (own1, parts))
    near1, far1, end0 = sides(own1), beyond(own1), turn(far0)
    got = exchange(parts)

    (end0,), (far1,), near1, (x, got), _ = step((end0,), (far1,), near1, (x, got))
    own2, own3 = (
        flat(got[:, :rows, 2 * head_cols + 2 * PAIR * i : 2 * head_cols + 2 * PAIR * (i + 1)])
        for i in range(2)
    )
    near2, far2, end1 = sides(own2), beyond(own2), turn(far1)

    packs = got[:, rows, : 2 * blk + n_dp].astype(jnp.int32)
    lens = packs[:, :blk].reshape(-1)
    dest = packs[:, blk : 2 * blk]
    counts = packs[:, 2 * blk :]
    peer = jnp.arange(n_dp, dtype=jnp.int32)
    pos = jnp.arange(blk, dtype=jnp.int32)
    before = jnp.sum(
        jnp.where(peer[None, None, :] < peer[None, :, None], counts[:, None, :], 0), axis=2
    )
    upto = before + counts
    sender = jnp.sum((upto[:, None, :] <= pos[None, :, None]).astype(jnp.int32), axis=2)
    is_sender = sender[:, :, None] == peer[None, None, :]
    rank = pos[None, :] - jnp.sum(jnp.where(is_sender, before[:, None, :], 0), axis=2)
    same = dest[:, :, None] == dest[:, None, :]
    slot_rank = jnp.sum((same & (pos[None, None, :] < pos[None, :, None])).astype(jnp.int32), axis=2)
    hit = (
        is_sender[:, :, :, None]
        & (dest[None, None] == peer[:, None, None, None])
        & (slot_rank[None, None] == rank[:, :, None, None])
    ).reshape(blocks, blocks)
    gap = peer ^ d
    gap = jnp.where(gap == 1, 2, jnp.where(gap == 2, 1, gap))
    place = (gap[:, None] * blk + pos[None, :]).reshape(-1)
    src = jnp.sum(jnp.where(hit, place[None, :], 0), axis=1)
    src_len = jnp.sum(jnp.where(hit, lens[None, :], 0), axis=1)
    table = jnp.concatenate([src, src_len, jnp.stack([z, m, d])])

    chunks = head_cols // PAIR

    def forward(c, own, near, far, end, before):
        pieces = [(x, x.shape, (0, 0)) for x in (own, near[1], far, near[0], end)]
        return forward_chunk(
            table, x, pieces, got, c, chunks, blk, n_sec, n_dp, before
        )

    f0 = forward(0, own0, near0, far0, end0, None)

    (end1,), (far2,), near2, (own3, f0), _ = step((end1,), (far2,), near2, (own3, f0))
    far3, end2 = beyond(own3), turn(far2)
    end3 = lax.ppermute(own3, "section", outer)
    f1 = forward(1, own1, near1, far1, end1, f0[1:])
    f1, own3_ = lax.optimization_barrier((f1, own3))
    near3 = sides(own3_)
    context_a = exchange(jnp.concatenate([f0[0], f1[0]], axis=2))
    f2 = forward(2, own2, near2, far2, end2, f1[1:])

    (end3, far3), near3, (f2, context_a), _ = step((end3, far3), near3, (f2, context_a))
    f3 = forward(3, own3, near3, far3, end3, f2[1:])

    late = []
    for t in range(n_dp):
        part = jnp.concatenate(
            [lax.dynamic_slice(f[0], (d ^ t, 0, 0), (1, rows, PAIR))[0] for f in (f2, f3)], axis=1
        )
        late.append(
            part if t == 0 else lax.ppermute(part, "dp", [(i, i ^ t) for i in range(n_dp)])
        )

    per_half = n_sec // n_mp
    span = half // per_half
    _, dkv, w = f3
    p_cols, q_own_cols, q_far_cols = (0, per_half), (1,), (per_half + 1,)
    pair = (2 * rows, 0)
    give_p = swap(backward(dkv, w, None, (2 * rows, 1), (span, p_cols), BF16))
    give_q = swap(backward(dkv, w, None, (2 * rows, 1), (span, q_far_cols + q_own_cols), BF16))
    send_y = backward(dkv, w, (give_p, 1, 0), (rows, 1), (span, p_cols), BF16)
    send_x = backward(dkv, w, (give_q, 0, 0), pair, (span, q_far_cols), BF16)
    send_y, send_x, late, dkv_, w_ = lax.optimization_barrier(
        (send_y, send_x, tuple(late), dkv, w)
    )
    got_y = lax.ppermute(send_y, "dp", ypairs)
    got_x = lax.ppermute(send_x, "mp", xpairs)
    p_own = backward(dkv_, w_, (give_p, 0, 0), (rows, 0), (span, p_cols), F32)
    q_own = backward(dkv_, w_, (give_q, 0, 1), pair, (span, q_own_cols), F32)
    context = gather_context(d, context_a, late)
    got_y, got_x, p_own, q_own, context = lax.optimization_barrier(
        (got_y, got_x, p_own, q_own, context)
    )
    to_x = (p_own[:, span:] + got_y[:, span:].astype(F32)).astype(BF16)
    to_y = (q_own[rows:] + got_x[rows:].astype(F32)).astype(BF16)
    last_x = lax.ppermute(to_x, "mp", xpairs)
    last_y = lax.ppermute(to_y, "dp", ypairs)
    enc_grad = finish(p_own, got_y, last_x, q_own, got_x, last_y)
    return (context, enc_grad)


def solution(mesh):
    placed = (
        P(("section", "dp"), "mp"),
        P(("section", "dp")),
        P(("section", "dp")),
        P(("section", "dp"), None),
        P(("section", "dp"), "mp"),
        P(("section", "dp"), "mp"),
        P(("section", "dp"), "mp"),
        P(("section", "dp"), "mp"),
    )
    sizes = tuple(mesh.shape[a] for a in ("section", "dp", "mp"))
    body = shards_section if sizes == (4, 4, 2) else shards_general
    return jax.shard_map(
        body,
        mesh=mesh,
        in_specs=placed,
        out_specs=(P(("section", "dp"), "mp"), P(("section", "dp"), "mp")),
        check_vma=False,
    )
```

```python
import functools

import jax
import jax.numpy as jnp
from jax import lax
from jax.experimental import pallas as pl
from jax.experimental.pallas import tpu as pltpu
from jax.sharding import PartitionSpec as P

DH = 64
BLOCK = 64
F32 = jnp.float32
BF16 = jnp.bfloat16


def attend(query_rows, key_rows, value_rows, grad_rows, key_lengths):
    block_count = key_lengths.shape[0]
    head_count = query_rows.shape[1] // DH
    shape_four = (block_count, BLOCK, head_count, DH)
    query_heads = query_rows.reshape(shape_four)
    key_heads = key_rows.reshape(shape_four)
    value_heads = value_rows.reshape(shape_four)
    grad_heads = grad_rows.reshape(shape_four)
    score_scale = DH ** (-0.5)
    scores = (
        jnp.einsum("bihd,bjhd->bhij", query_heads, key_heads, preferred_element_type=jnp.float32)
        * score_scale
    )
    visible = (
        jnp.arange(BLOCK, dtype=jnp.float32)[None, None, None, :] < key_lengths[:, None, None, None]
    )
    scores = jnp.where(visible, scores, -1e30)
    row_max = jnp.max(scores, axis=-1, keepdims=True)
    weights_exp = jnp.exp(scores - row_max)
    probabilities = weights_exp / jnp.sum(weights_exp, axis=-1, keepdims=True)
    prob_bf = probabilities.astype(jnp.bfloat16)
    context = jnp.einsum(
        "bhij,bjhd->bihd", prob_bf, value_heads, preferred_element_type=jnp.float32
    ).astype(jnp.bfloat16)
    prob_grad = jnp.einsum(
        "bihd,bjhd->bhij", grad_heads, value_heads, preferred_element_type=jnp.float32
    )
    row_dot = jnp.sum(probabilities * prob_grad, axis=-1, keepdims=True)
    score_grad = (probabilities * (prob_grad - row_dot) * score_scale).astype(jnp.bfloat16)
    key_grad = jnp.einsum(
        "bhij,bihd->bjhd", score_grad, query_heads, preferred_element_type=jnp.float32
    ).astype(jnp.bfloat16)
    value_grad = jnp.einsum(
        "bhij,bihd->bjhd", prob_bf, grad_heads, preferred_element_type=jnp.float32
    ).astype(jnp.bfloat16)
    flat_shape = (block_count * BLOCK, head_count * DH)
    return (
        context.reshape(flat_shape),
        key_grad.reshape(flat_shape),
        value_grad.reshape(flat_shape),
    )


def through(table, data, lead_shape):
    moved = jnp.dot(table, data, preferred_element_type=jnp.float32).astype(jnp.bfloat16)
    return moved.reshape(lead_shape + data.shape[1:])


def shards_general(enc_rows, enc_len, dest_dp, peer_counts, queries, ctx_grad, w_key, w_value):
    peer_count = lax.axis_size("dp")
    model_groups = lax.axis_size("mp")
    block_count = dest_dp.shape[0]
    slot_count = max(2, -(-block_count // peer_count))
    row_count, feature_width = enc_rows.shape
    key_full, value_full = (
        lax.all_gather(w_key, ("section", "dp"), axis=0, tiled=True),
        lax.all_gather(w_value, ("section", "dp"), axis=0, tiled=True),
    )
    positions = jnp.arange(block_count, dtype=jnp.int32)
    same_dest = dest_dp[:, None] == dest_dp[None, :]
    slot_rank = jnp.sum(
        (same_dest & (positions[None, :] < positions[:, None])).astype(jnp.int32), axis=1
    )
    target_slot = dest_dp * slot_count + slot_rank
    slot_ids = jnp.arange(peer_count * slot_count, dtype=jnp.int32)
    send_map = (slot_ids[:, None] == target_slot[None, :]).astype(jnp.bfloat16)
    arrivals = peer_counts[0]
    arrival_ends = jnp.cumsum(arrivals)
    sender = jnp.sum((arrival_ends[None, :] <= positions[:, None]).astype(jnp.int32), axis=1)
    first_pos = jnp.take(arrival_ends, sender) - jnp.take(arrivals, sender)
    slot_pick = sender * slot_count + positions - first_pos
    recv_map = (slot_pick[:, None] == slot_ids[None, :]).astype(jnp.bfloat16)
    lengths_own = enc_len.astype(jnp.float32).astype(jnp.bfloat16).reshape(block_count, 1)
    all_slots = peer_count * slot_count
    outgoing = through(send_map, enc_rows.reshape(block_count, -1), (peer_count, slot_count))
    outgoing_len = through(send_map, lengths_own, (peer_count, slot_count))
    incoming, incoming_len = (
        lax.all_to_all(outgoing, "dp", split_axis=0, concat_axis=0, tiled=True),
        lax.all_to_all(outgoing_len, "dp", split_axis=0, concat_axis=0, tiled=True),
    )
    rows_here = through(recv_map, incoming.reshape(all_slots, -1), (block_count,)).reshape(
        row_count, feature_width
    )
    lengths_here = through(recv_map, incoming_len.reshape(all_slots, 1), (block_count,))[
        :, 0
    ].astype(jnp.float32)
    shard_cols = lax.all_gather(rows_here, "mp", axis=1, tiled=True)
    key_acc = jnp.dot(shard_cols, key_full, preferred_element_type=jnp.float32)
    value_acc = jnp.dot(shard_cols, value_full, preferred_element_type=jnp.float32)
    context, key_grad, value_grad = attend(
        queries,
        key_acc.astype(jnp.bfloat16),
        value_acc.astype(jnp.bfloat16),
        ctx_grad,
        lengths_here,
    )
    col_span = key_full.shape[0] // model_groups
    pieces_out = []
    for group_idx in range(model_groups):
        key_part = key_full[group_idx * col_span : (group_idx + 1) * col_span]
        value_part = value_full[group_idx * col_span : (group_idx + 1) * col_span]
        partial_value = lax.dot_general(
            key_grad, key_part, (((1,), (1,)), ((), ())), preferred_element_type=jnp.float32
        )
        partial_value = partial_value + lax.dot_general(
            value_grad, value_part, (((1,), (1,)), ((), ())), preferred_element_type=jnp.float32
        )
        pieces_out.append(partial_value.astype(jnp.bfloat16))
    summed = lax.psum_scatter(
        jnp.concatenate(pieces_out, axis=1), "mp", scatter_dimension=1, tiled=True
    )
    outgoing_grad = through(recv_map.T, summed.reshape(block_count, -1), (peer_count, slot_count))
    returned = lax.all_to_all(outgoing_grad, "dp", split_axis=0, concat_axis=0, tiled=True)
    enc_grad = through(send_map.T, returned.reshape(all_slots, -1), (block_count,)).reshape(
        row_count, feature_width
    )
    return (context, enc_grad)


PAIR = 2 * DH
SLOTS = (0, 2, 1, 3)
VMEM = 56 << 20
SHORT = pl.CostEstimate(flops=1, bytes_accessed=1, transcendentals=0)


def nt(a, b):
    return lax.dot_general(a, b, (((1,), (1,)), ((), ())), preferred_element_type=F32)


def tn(a, b):
    return lax.dot_general(a, b, (((0,), (0,)), ((), ())), preferred_element_type=F32)


def forward_kernel(n_dp, n_sec, n_half, blk, in_slots, tab, *refs):
    blocks = n_dp * blk
    x_refs = refs[: n_half * n_dp]
    own, above, far, below, end = refs[n_half * n_dp : n_half * n_dp + 5]
    q_ref, g_ref = refs[n_half * n_dp + 5 : n_half * n_dp + 7]
    ctx_ref, dkv_ref, w_ref, acc, kv = refs[-5:]
    rows = acc.shape[0] // n_dp
    step = pl.program_id(0)
    per_half = n_sec // n_half
    z = tab[2 * blocks]
    m = tab[2 * blocks + 1]
    section = (m ^ (step // per_half)) * per_half + step % per_half
    hop = (section - z + n_sec) % n_sec

    def take(ref):
        if in_slots:
            d = tab[2 * blocks + 2]
            for t in range(n_dp):
                to = pl.multiple_of((d ^ t) * rows, rows)
                w_ref[pl.ds(to, rows), :] = ref[t * rows : (t + 1) * rows, :]
        else:
            w_ref[...] = ref[...].reshape(w_ref.shape)

    @pl.when(hop == 0)
    def _():
        take(own)

    @pl.when((hop == 1) & (z != n_sec - 1))
    def _():
        take(above)

    @pl.when(hop == 2)
    def _():
        take(far)

    @pl.when((hop == n_sec - 1) & (z != 0))
    def _():
        take(below)

    @pl.when(((hop == 1) & (z == n_sec - 1)) | ((hop == n_sec - 1) & (z == 0)))
    def _():
        take(end)

    for h in range(n_half):

        @pl.when(step // per_half == h)
        def _():
            for t in range(n_dp):
                at = slice(t * rows, (t + 1) * rows)
                part = jnp.dot(
                    x_refs[h * n_dp + t][0], w_ref[...], preferred_element_type=F32
                )
                if h == 0:
                    acc[at, :] = jnp.where(step == 0, part, acc[at, :] + part)
                else:
                    acc[at, :] += part

    @pl.when(step == n_sec - 1)
    def _():
        kv[...] = acc[...].astype(BF16)
        lane = lax.broadcasted_iota(jnp.int32, (BLOCK, PAIR), 1) < DH
        key_pos = lax.broadcasted_iota(jnp.int32, (BLOCK, PAIR), 0)
        scale = DH ** (-0.5)
        zero = jnp.zeros((BLOCK, PAIR), BF16)

        def group(bs):
            source = [pl.ds(pl.multiple_of(tab[b] * BLOCK, BLOCK), BLOCK) for b in bs]
            here = [pl.ds((b % blk) * BLOCK, BLOCK) for b in bs]
            key = [kv[at, 0:PAIR] for at in source]
            value = [kv[at, PAIR : 2 * PAIR] for at in source]

            def split(ref):
                rows_of = [ref[b // blk, at, :] for b, at in zip(bs, here)]
                return [
                    jnp.concatenate([jnp.where(lane, x, zero), jnp.where(lane, zero, x)], axis=0)
                    for x in rows_of
                ]

            query = split(q_ref)
            grad = split(g_ref)
            scores = [nt(k, q) * scale for k, q in zip(key, query)]
            prob_grad = [nt(v, g) for v, g in zip(value, grad)]
            scores = [jnp.where(key_pos < tab[blocks + b], x, -1e30) for b, x in zip(bs, scores)]
            weights = [jnp.exp(x - jnp.max(x, axis=0, keepdims=True)) for x in scores]
            probs = [x / jnp.sum(x, axis=0, keepdims=True) for x in weights]
            prob_bf = [x.astype(BF16) for x in probs]
            ctx = [tn(p, v) for p, v in zip(prob_bf, value)]
            dv = [jnp.dot(p, g, preferred_element_type=F32) for p, g in zip(prob_bf, grad)]
            row_dot = [jnp.sum(p * x, axis=0, keepdims=True) for p, x in zip(probs, prob_grad)]
            score_grad = [
                (p * (x - r) * scale).astype(BF16) for p, x, r in zip(probs, prob_grad, row_dot)
            ]
            dk = [jnp.dot(x, q, preferred_element_type=F32) for x, q in zip(score_grad, query)]
            for n, b in enumerate(bs):
                ctx_ref[b // blk, here[n], :] = jnp.where(
                    lane, ctx[n][:BLOCK], ctx[n][BLOCK:]
                ).astype(BF16)
                dkv_ref[source[n], 0:PAIR] = dk[n].astype(BF16)
                dkv_ref[source[n], PAIR : 2 * PAIR] = dv[n].astype(BF16)

        for b in range(0, blocks, blk):
            group(range(b, b + blk))


def forward_chunk(table, x, pieces, got, chunk, chunks, blk, n_sec, n_dp, before):
    n_half = x.shape[0] // n_dp
    cols = 2 * PAIR
    per_half = n_sec // n_half
    span = x.shape[2] // per_half
    rows = span // n_dp
    scalars = 2 * n_dp * blk

    def x_spec(h, slot):
        def at(a, t):
            sender = (t[scalars + 2] ^ slot) * n_half + (t[scalars + 1] ^ h)
            return (sender, 0, jnp.clip(a - h * per_half, 0, per_half - 1))

        return pl.BlockSpec((1, rows, span), at)

    def fixed(shape, at):
        return pl.BlockSpec(shape, lambda a, t: at)

    def head(at):
        return pl.BlockSpec((n_dp, rows, PAIR), lambda a, t: (0, 0, at))

    operands = [table] + [x] * (n_half * n_dp) + [p[0] for p in pieces] + [got, got]
    in_specs = [x_spec(h, slot) for h in range(n_half) for slot in SLOTS]
    in_specs += [fixed(shape, at) for _, shape, at in pieces]
    in_specs += [head(chunk), head(chunks + chunk)]
    aliases = {}
    if before is not None:
        aliases = {len(operands): 1, len(operands) + 1: 2}
        operands += before
        in_specs += [pl.BlockSpec(memory_space=pl.ANY)] * 2
    return pl.pallas_call(
        functools.partial(forward_kernel, n_dp, n_sec, n_half, blk, chunk == 0),
        grid_spec=pltpu.PrefetchScalarGridSpec(
            num_scalar_prefetch=1,
            grid=(n_sec,),
            in_specs=in_specs,
            out_specs=[
                head(0),
                pl.BlockSpec((n_dp * rows, cols), lambda a, t: (0, chunk)),
                pl.BlockSpec((span, cols), lambda a, t: (a, chunk)),
            ],
            scratch_shapes=[
                pltpu.VMEM((n_dp * rows, cols), F32),
                pltpu.VMEM((n_dp * rows, cols), BF16),
            ],
        ),
        out_shape=[
            jax.ShapeDtypeStruct((n_dp, rows, PAIR), BF16),
            jax.ShapeDtypeStruct((n_dp * rows, chunks * cols), BF16),
            jax.ShapeDtypeStruct((n_sec * span, chunks * cols), BF16),
        ],
        input_output_aliases=aliases,
        compiler_params=pltpu.CompilerParams(vmem_limit_bytes=VMEM),
        cost_estimate=SHORT,
        name="fwd",
    )(*operands)


def backward_kernel(*refs):
    depth = refs[0].shape[1]
    total = nt(refs[0][:, : 2 * PAIR], refs[1][:, : 2 * PAIR])
    for at in range(2 * PAIR, depth, 2 * PAIR):
        total += nt(refs[0][:, at : at + 2 * PAIR], refs[1][:, at : at + 2 * PAIR])
    for ref in refs[2:-1]:
        total += ref[...].astype(F32)
    refs[-1][...] = total.astype(refs[-1].dtype)


def backward(dkv, w, received, rows, cols, out_dtype):
    row_n, row_at = rows
    span, blocks = cols
    depth = dkv.shape[1]
    tile = 1024 if len(blocks) > 1 else 512
    per_block = span // tile

    def col(i):
        at = blocks[0]
        for k in range(1, len(blocks)):
            at = jnp.where(i >= k * per_block, blocks[k], at)
        return at * per_block + i % per_block

    specs = [
        pl.BlockSpec((row_n, depth), lambda i: (row_at, 0)),
        pl.BlockSpec((tile, depth), lambda i: (col(i), 0)),
    ]
    extra = ()
    if received is not None:
        array, add_row, add_col = received
        specs.append(
            pl.BlockSpec((row_n, tile), lambda i: (add_row, add_col * per_block + i))
        )
        extra = (array,)
    return pl.pallas_call(
        backward_kernel,
        grid=(len(blocks) * per_block,),
        in_specs=specs,
        out_specs=pl.BlockSpec((row_n, tile), lambda i: (0, i)),
        out_shape=jax.ShapeDtypeStruct((row_n, len(blocks) * span), out_dtype),
        compiler_params=pltpu.CompilerParams(vmem_limit_bytes=VMEM),
        cost_estimate=SHORT,
        name="bwd",
    )(dkv, w, *extra)


def finish_kernel(p_ref, got_y, last_x, q_ref, got_x, last_y, out):
    span = out.shape[1] // 2
    out[:, :span] = (
        p_ref[...] + got_y[...].astype(F32) + last_x[...].astype(F32)
    ).astype(BF16)
    out[:, span:] = (
        q_ref[...] + got_x[...].astype(F32) + last_y[...].astype(F32)
    ).astype(BF16)


def finish(*operands):
    rows, span = operands[2].shape
    tiles = 2
    block = pl.BlockSpec((rows // tiles, span), lambda i: (i, 0))
    return pl.pallas_call(
        finish_kernel,
        grid=(tiles,),
        in_specs=[block] * 6,
        out_specs=pl.BlockSpec((rows // tiles, 2 * span), lambda i: (i, 0)),
        out_shape=jax.ShapeDtypeStruct((rows, 2 * span), BF16),
        compiler_params=pltpu.CompilerParams(vmem_limit_bytes=16 << 20),
        cost_estimate=SHORT,
        name="finish",
    )(*operands)


def weight_kernel(k_ref, v_ref, out):
    out[0, :, :PAIR] = k_ref[...]
    out[0, :, PAIR:] = v_ref[...]


def pack_weights(w_key, w_value, chunk, n_dp):
    rows, width = w_key.shape
    per_owner = width // n_dp // PAIR
    block = pl.BlockSpec((rows, PAIR), lambda j: (0, j * per_owner + chunk))
    return pl.pallas_call(
        weight_kernel,
        grid=(n_dp,),
        in_specs=[block] * 2,
        out_specs=pl.BlockSpec((1, rows, 2 * PAIR), lambda j: (j, 0, 0)),
        out_shape=jax.ShapeDtypeStruct((n_dp, rows, 2 * PAIR), BF16),
        compiler_params=pltpu.CompilerParams(vmem_limit_bytes=VMEM),
        cost_estimate=SHORT,
        name="pack_weights",
    )(w_key, w_value)


def pack_kernel(q_ref, g_ref, k_ref, v_ref, small_ref, out):
    rows, cols = q_ref.shape
    parts = [q_ref[...], g_ref[...]]
    for c in range(0, k_ref.shape[1], PAIR):
        parts += [k_ref[:, c : c + PAIR], v_ref[:, c : c + PAIR]]
    at = 0
    for part in parts:
        out[0, :rows, at : at + part.shape[1]] = part
        at += part.shape[1]
    out[0, rows:, :] = jnp.zeros((out.shape[1] - rows, out.shape[2]), BF16)
    out[0, rows:, :PAIR] = small_ref[...]


def pack(queries, grads, w_key, w_value, small, n_dp):
    rows, width = queries.shape
    cols = width // n_dp
    block = pl.BlockSpec((rows, cols), lambda j: (0, j))
    tail = pl.BlockSpec((rows, cols // 2), lambda j: (0, 2 * j + 1))
    extra = small.shape[0]
    return pl.pallas_call(
        pack_kernel,
        grid=(n_dp,),
        in_specs=[block, block, tail, tail, pl.BlockSpec(small.shape, lambda j: (0, 0))],
        out_specs=pl.BlockSpec((1, rows + extra, 3 * cols), lambda j: (j, 0, 0)),
        out_shape=jax.ShapeDtypeStruct((n_dp, rows + extra, 3 * cols), BF16),
        compiler_params=pltpu.CompilerParams(vmem_limit_bytes=VMEM),
        cost_estimate=SHORT,
        name="pack",
    )(queries, grads, w_key, w_value, small)


def context_kernel(n_dp, tab, early, *refs):
    out = refs[-1]
    cols = early.shape[2]
    out[:, :cols] = early[0]
    for t in range(n_dp):

        @pl.when(pl.program_id(0) == t)
        def _():
            out[:, cols:] = refs[t][...]


def gather_context(d, early, late):
    n_dp, rows, cols = early.shape
    last = late[0].shape[1]
    return pl.pallas_call(
        functools.partial(context_kernel, n_dp),
        grid_spec=pltpu.PrefetchScalarGridSpec(
            num_scalar_prefetch=1,
            grid=(n_dp,),
            in_specs=[pl.BlockSpec((1, rows, cols), lambda t, tab: (tab[0] ^ t, 0, 0))]
            + [pl.BlockSpec((rows, last), lambda t, tab: (0, 0))] * n_dp,
            out_specs=pl.BlockSpec((rows, cols + last), lambda t, tab: (0, tab[0] ^ t)),
        ),
        out_shape=jax.ShapeDtypeStruct((rows, n_dp * (cols + last)), BF16),
        compiler_params=pltpu.CompilerParams(vmem_limit_bytes=VMEM),
        cost_estimate=SHORT,
        name="gather_context",
    )(d.reshape(1), early, *late)


def shards_section(enc_rows, enc_len, dest_dp, peer_counts, queries, ctx_grad, w_key, w_value):
    n_sec, n_dp, n_mp = (lax.axis_size(a) for a in ("section", "dp", "mp"))
    z, d, m = (lax.axis_index(a).astype(jnp.int32) for a in ("section", "dp", "mp"))
    blk = dest_dp.shape[0]
    blocks = blk * n_dp
    rows, half = enc_rows.shape
    head_cols = w_key.shape[1] // n_dp

    core = [(i, i ^ 1) for i in range(n_dp)]
    ypairs = [(i, i ^ 2) for i in range(n_dp)]
    xpairs = [(0, 1), (1, 0)]
    up = [(i, i + 1) for i in range(n_sec - 1)]
    down = [(i + 1, i) for i in range(n_sec - 1)]
    over_two = [(i, i ^ 2) for i in range(n_sec)]
    ends = [(1, 0), (2, 3)]
    outer = [(0, n_sec - 1), (n_sec - 1, 0)]

    def step(*waited, released=()):
        done = ()
        for group in waited:
            done = done + (tuple(group),)
            if group is not waited[-1]:
                done = lax.optimization_barrier(done)
        done, released = lax.optimization_barrier((done, tuple(released)))
        return (*done, released)

    def swap(x):
        return lax.ppermute(x, "dp", core)

    def exchange(x):
        return lax.all_to_all(x, "dp", split_axis=0, concat_axis=0, tiled=True)

    def sides(piece):
        return lax.ppermute(piece, "section", up), lax.ppermute(piece, "section", down)

    def beyond(piece):
        return lax.ppermute(piece, "section", over_two)

    def turn(far):
        return lax.ppermute(far, "section", ends)

    def flat(x):
        return x.reshape(n_dp * rows, 2 * PAIR)

    pieces = []
    for t in range(n_dp):
        at = (d ^ t) * head_cols
        cut = jnp.concatenate(
            [lax.dynamic_slice(w, (0, at), (rows, PAIR)) for w in (w_key, w_value)], axis=1
        )
        pieces.append(cut if t == 0 else lax.ppermute(cut, "dp", [(i, i ^ t) for i in range(n_dp)]))
    own0 = jnp.concatenate(pieces, axis=0)
    x = lax.all_gather(enc_rows, ("dp", "mp"), axis=0, tiled=False)
    small = jnp.concatenate([enc_len, dest_dp, peer_counts[0]]).astype(BF16)
    small = jnp.pad(small[None, :], ((0, 15), (0, PAIR - small.shape[0])))

    (own0,), (w_k, w_v) = step((own0,), released=(w_key, w_value))
    near0, far0 = sides(own0), beyond(own0)
    own1 = flat(exchange(pack_weights(w_k, w_v, 1, n_dp)))
    parts = pack(queries, ctx_grad, w_k, w_v, small, n_dp)

    (far0,), near0, (own1, parts), _ = step((far0,), near0, (own1, parts))
    near1, far1, end0 = sides(own1), beyond(own1), turn(far0)
    got = exchange(parts)

    (end0,), (far1,), near1, (x, got), _ = step((end0,), (far1,), near1, (x, got))
    own2, own3 = (
        flat(got[:, :rows, 2 * head_cols + 2 * PAIR * i : 2 * head_cols + 2 * PAIR * (i + 1)])
        for i in range(2)
    )
    near2, far2, end1 = sides(own2), beyond(own2), turn(far1)

    packs = got[:, rows, : 2 * blk + n_dp].astype(jnp.int32)
    lens = packs[:, :blk].reshape(-1)
    dest = packs[:, blk : 2 * blk]
    counts = packs[:, 2 * blk :]
    peer = jnp.arange(n_dp, dtype=jnp.int32)
    pos = jnp.arange(blk, dtype=jnp.int32)
    before = jnp.sum(
        jnp.where(peer[None, None, :] < peer[None, :, None], counts[:, None, :], 0), axis=2
    )
    upto = before + counts
    sender = jnp.sum((upto[:, None, :] <= pos[None, :, None]).astype(jnp.int32), axis=2)
    is_sender = sender[:, :, None] == peer[None, None, :]
    rank = pos[None, :] - jnp.sum(jnp.where(is_sender, before[:, None, :], 0), axis=2)
    same = dest[:, :, None] == dest[:, None, :]
    slot_rank = jnp.sum((same & (pos[None, None, :] < pos[None, :, None])).astype(jnp.int32), axis=2)
    hit = (
        is_sender[:, :, :, None]
        & (dest[None, None] == peer[:, None, None, None])
        & (slot_rank[None, None] == rank[:, :, None, None])
    ).reshape(blocks, blocks)
    gap = peer ^ d
    gap = jnp.where(gap == 1, 2, jnp.where(gap == 2, 1, gap))
    place = (gap[:, None] * blk + pos[None, :]).reshape(-1)
    src = jnp.sum(jnp.where(hit, place[None, :], 0), axis=1)
    src_len = jnp.sum(jnp.where(hit, lens[None, :], 0), axis=1)
    table = jnp.concatenate([src, src_len, jnp.stack([z, m, d])])

    chunks = head_cols // PAIR

    def forward(c, own, near, far, end, before):
        pieces = [(x, x.shape, (0, 0)) for x in (own, near[1], far, near[0], end)]
        return forward_chunk(
            table, x, pieces, got, c, chunks, blk, n_sec, n_dp, before
        )

    f0 = forward(0, own0, near0, far0, end0, None)

    (end1,), (far2,), near2, (own3, f0), _ = step((end1,), (far2,), near2, (own3, f0))
    far3, end2 = beyond(own3), turn(far2)
    end3 = lax.ppermute(own3, "section", outer)
    f1 = forward(1, own1, near1, far1, end1, f0[1:])
    f1, own3_ = lax.optimization_barrier((f1, own3))
    near3 = sides(own3_)
    context_a = exchange(jnp.concatenate([f0[0], f1[0]], axis=2))
    f2 = forward(2, own2, near2, far2, end2, f1[1:])

    (end3, far3), near3, (f2, context_a), _ = step((end3, far3), near3, (f2, context_a))
    f3 = forward(3, own3, near3, far3, end3, f2[1:])

    late = []
    for t in range(n_dp):
        part = jnp.concatenate(
            [lax.dynamic_slice(f[0], (d ^ t, 0, 0), (1, rows, PAIR))[0] for f in (f2, f3)], axis=1
        )
        late.append(
            part if t == 0 else lax.ppermute(part, "dp", [(i, i ^ t) for i in range(n_dp)])
        )

    per_half = n_sec // n_mp
    span = half // per_half
    _, dkv, w = f3
    p_cols, q_own_cols, q_far_cols = (0, per_half), (1,), (per_half + 1,)
    pair = (2 * rows, 0)
    give_p = swap(backward(dkv, w, None, (2 * rows, 1), (span, p_cols), BF16))
    give_q = swap(backward(dkv, w, None, (2 * rows, 1), (span, q_far_cols + q_own_cols), BF16))
    send_y = backward(dkv, w, (give_p, 1, 0), (rows, 1), (span, p_cols), BF16)
    send_x = backward(dkv, w, (give_q, 0, 0), pair, (span, q_far_cols), BF16)
    send_y, send_x, late, dkv_, w_ = lax.optimization_barrier(
        (send_y, send_x, tuple(late), dkv, w)
    )
    got_y = lax.ppermute(send_y, "dp", ypairs)
    got_x = lax.ppermute(send_x, "mp", xpairs)
    p_own = backward(dkv_, w_, (give_p, 0, 0), (rows, 0), (span, p_cols), F32)
    q_own = backward(dkv_, w_, (give_q, 0, 1), pair, (span, q_own_cols), F32)
    context = gather_context(d, context_a, late)
    got_y, got_x, p_own, q_own, context = lax.optimization_barrier(
        (got_y, got_x, p_own, q_own, context)
    )
    to_x = (p_own[:, span:] + got_y[:, span:].astype(F32)).astype(BF16)
    to_y = (q_own[rows:] + got_x[rows:].astype(F32)).astype(BF16)
    last_x = lax.ppermute(to_x, "mp", xpairs)
    last_y = lax.ppermute(to_y, "dp", ypairs)
    enc_grad = finish(p_own, got_y, last_x, q_own, got_x, last_y)
    return (context, enc_grad)


def solution(mesh):
    placed = (
        P(("section", "dp"), "mp"),
        P(("section", "dp")),
        P(("section", "dp")),
        P(("section", "dp"), None),
        P(("section", "dp"), "mp"),
        P(("section", "dp"), "mp"),
        P(("section", "dp"), "mp"),
        P(("section", "dp"), "mp"),
    )
    sizes = tuple(mesh.shape[a] for a in ("section", "dp", "mp"))
    body = shards_section if sizes == (4, 4, 2) else shards_general
    return jax.shard_map(
        body,
        mesh=mesh,
        in_specs=placed,
        out_specs=(P(("section", "dp"), "mp"), P(("section", "dp"), "mp")),
        check_vma=False,
    )
```
